256 devices in a mesh: dp: 16 (over y, z_lo, core), expert: 16 (over z_hi, x).
Axes of the slice: x: 4, y: 4, z: 8 (z_hi: 4, z_lo: 2; z = z_hi * 2 + z_lo), core: 2. Of those that a mesh axis runs over, the one named last changes fastest.
Arguments:
- tokens: bfloat16 [16384, 7168], P('expert', 'dp'), may hold values from -6 to 6
- expert_ids: int32 [16384, 8], P('expert'), may hold values from 0 to 255, all different within a row; in each aligned block of 1024 rows (0 to 1023, 1024 to 2047, ...) at most 64 rows name the same one
- gates: float32 [16384, 8], P('expert'), may hold values from 0.05 to 1
- gate_weight: bfloat16 [16, 7168, 2048], P('expert', 'dp'), may hold values from -0.0625 to 0.0625
- up_weight: bfloat16 [16, 7168, 2048], P('expert', 'dp'), may hold values from -0.0625 to 0.0625
- down_weight: bfloat16 [16, 2048, 7168], P('expert', None, 'dp'), may hold values from -0.125 to 0.125
- partner: int32 [16], replicated, may hold values from 0 to 15, as said below
- capacity: int32 [16], replicated, may hold values from 80 to 640, as said below
Outputs:
- mixed: bfloat16 [16384, 7168], P('expert', 'dp')
- placed_gate: bfloat16 [16, 7168, 2048], P('expert', 'dp')
- placed_up: bfloat16 [16, 7168, 2048], P('expert', 'dp')
- placed_down: bfloat16 [16, 2048, 7168], P('expert', None, 'dp')
The draws below stay inside these ranges and needn't reach their ends.
Inputs may be any that keep to these rules, and one draw needn't show every extreme that they name: `expert_ids`: in every aligned block of 1024 rows no expert number is named by more than 64 rows. partner[partner[k]] == k for every slot k; 4 pairs of slots are exchanged, the other slots map to themselves. Some slot has capacity exactly 640.
All inputs are finite; a program needn't handle non-finite values.
Results may differ from the reference program's by a relative error of at most 0.0057.
Values may be sent and summed in bfloat16 or wider, within the bound.
A program may use at most 128 MiB of HBM per device.

```python
import math
import jax
import jax.numpy as jnp
import numpy as np
from jax import lax

D = 7168
FF = 2048
EXPERTS = 256
TOP = 8
TOK_DEV = 1024
MOST = 64
CAP_MAX = 640
TOKENS = 16384
N_EXPERT = 16


def draw_partner(key, part):
    order = jax.random.permutation(key, N_EXPERT).astype(jnp.int32)
    pair_count = N_EXPERT // 4
    result = jnp.arange(N_EXPERT, dtype=jnp.int32)
    first_half = order[0:2 * pair_count:2]
    second_half = order[1:2 * pair_count:2]
    result = result.at[first_half].set(second_half).at[second_half].set(first_half)
    return result


def draw_capacity(key, part):
    key_one, key_two = jax.random.split(jax.random.fold_in(key, 7))
    values = jax.random.randint(key_one, (N_EXPERT,), CAP_MAX // 8, CAP_MAX + 1)
    full_slot = jax.random.randint(key_two, (), 0, N_EXPERT)
    return values.at[full_slot].set(CAP_MAX).astype(jnp.int32)


def level_of(own_key, dims, pieces, least, top_value):
    def one(position, blocks):
        heights = jax.random.uniform(jax.random.fold_in(jax.random.fold_in(own_key, 6), position), (blocks,), jnp.float32, least / len(pieces), top_value / len(pieces))
        return jnp.repeat(jnp.exp(heights), dims[position] // blocks).reshape((-1,) + (1,) * (len(dims) - position - 1))

    gain = one(*pieces[0])
    for cut in pieces[1:]:
        gain = gain * one(*cut)
    return gain


def shared_out(own_key, own, number, rows, amount, top, reach, lean):
    sequence = jax.random.permutation(own_key, amount)
    packed, common = load_shares(amount, rows * top, reach, lean, True), load_shares(amount, rows * top, reach, lean, False)
    places = jnp.arange(amount)

    def named(sizes, offset_by):
        used = int((sizes > 0).sum())
        fixed = max(1, used // 4)
        shifted = fixed + (places - fixed + offset_by * (used - fixed)) % max(1, amount - fixed)
        return jnp.zeros((amount,), jnp.int32).at[sequence[jnp.where(places < fixed, places, shifted)]].set(jnp.asarray(sizes, jnp.int32))

    sizes = jnp.where(number % 4 == 0, named(packed, number // 4), named(common, number - number // 4 - 1))
    mixed = jax.random.permutation(jax.random.fold_in(own, 3), amount)
    source_of, sink = mixed[0:amount // 2 * 2:2], mixed[1:amount // 2 * 2:2]
    slack = jnp.minimum(sizes[source_of] - 1, reach - sizes[sink]) // 2
    slack = jnp.where((source_of == sequence[0]) | (sink == sequence[0]) | (sizes[sink] == 0), 0, jnp.maximum(slack, 0))
    shifted = jax.random.randint(jax.random.fold_in(own, 4), (amount // 2,), 0, 1 << 20) % (slack + 1)
    sizes = sizes.at[source_of].add(-shifted).at[sink].add(shifted)
    members = jnp.searchsorted(jnp.cumsum(sizes), jnp.arange(rows * top), side="right").astype(jnp.int32)
    listing = members.reshape(top, rows).T
    listing = listing[jax.random.permutation(jax.random.fold_in(own, 1), rows)]
    offset_by = jax.random.randint(jax.random.fold_in(own, 2), (rows, 1), 0, top)
    return jnp.take_along_axis(listing, (jnp.arange(top)[None, :] + offset_by) % top, axis=1)


def load_shares(amount, total, bound, slope, full):
    loads = [(1 << 20) // math.isqrt(rank ** slope) + 1 for rank in range(1, amount + 1)]
    largest = bound if full else min(bound, max(-(-total // amount), total * loads[0] // sum(loads)))
    least = 1 if total - largest >= amount - 1 else 0
    given, surplus = [largest] + [least] * (amount - 1), total - largest - least * (amount - 1)
    while surplus > 0:
        candidates = [i for i in range(1, amount) if given[i] < largest] or [i for i in range(1, amount) if given[i] < bound]
        mass, budget = sum([loads[i] for i in candidates]), surplus
        for i in candidates:
            more = min(bound - given[i], max(1, budget * loads[i] // mass), surplus)
            given[i] = given[i] + more
            surplus = surplus - more
    return np.array(given)


def bell_draw(stream_key, dims, spread, limit, cuts=(), kind=jnp.bfloat16):
    array = spread * jax.random.normal(stream_key, dims, jnp.float32)
    if cuts:
        array = array * level_of(stream_key, dims, cuts, -0.22, 0.18)
    return jnp.clip(array, -limit, limit).astype(kind)


def setup_inputs(seed: int = 0) -> dict:
    key_list = jax.random.split(jax.random.key(seed), 9)
    tokens = bell_draw(key_list[0], (TOKENS, D), 1.0, 6.0, ((0, 16), (1, 16)))
    expert_ids_keys = jax.random.split(jax.random.fold_in(key_list[1], 1), TOKENS // TOK_DEV)
    expert_ids_turns = jax.random.permutation(jax.random.fold_in(key_list[1], 3), TOKENS // TOK_DEV)
    expert_ids = jax.vmap(lambda own, number: shared_out(jax.random.fold_in(key_list[1], 2), own, number, TOK_DEV, EXPERTS, TOP, MOST, 2))(expert_ids_keys, expert_ids_turns).reshape((TOKENS, TOP))
    gates = jnp.clip(0.05 + 0.95 * jax.random.uniform(key_list[2], (TOKENS, TOP), jnp.float32) ** level_of(key_list[2], (TOKENS, TOP), ((0, 16),), -0.2, 0.2), 0.05, 1.0)
    gate_weight = bell_draw(key_list[3], (N_EXPERT, D, FF), D ** -0.5, 0.0625, ((0, 16), (1, 16)))
    up_weight = bell_draw(key_list[4], (N_EXPERT, D, FF), D ** -0.5, 0.0625, ((0, 16), (1, 16)))
    down_weight = bell_draw(key_list[5], (N_EXPERT, FF, D), FF ** -0.5, 0.125, ((0, 16), (2, 16)))
    partner = draw_partner(jax.random.fold_in(key_list[8], 71), 0)
    capacity = draw_capacity(jax.random.fold_in(key_list[8], 71), 0)
    return dict(tokens=tokens, expert_ids=expert_ids, gates=gates, gate_weight=gate_weight, up_weight=up_weight, down_weight=down_weight, partner=partner, capacity=capacity)


def reference(tokens, expert_ids, gates, gate_weight, up_weight, down_weight, partner, capacity):
    flat_ids = expert_ids.reshape(-1)
    flat_rows = (jnp.arange(flat_ids.shape[0], dtype=jnp.int32) // TOP).astype(jnp.int32)
    flat_gates = gates.reshape(-1)
    experts = jnp.arange(N_EXPERT, dtype=jnp.int32)
    limits = capacity[partner]

    def one_expert(running, inputs):
        expert, cap_limit, w_gate, w_up, w_down = inputs
        chosen = flat_ids == expert
        rank_list = jnp.cumsum(chosen.astype(jnp.int32)) - 1
        kept_mask = chosen & (rank_list < cap_limit)
        slot_place = jnp.where(kept_mask, rank_list, CAP_MAX).astype(jnp.int32)
        slot_rows = jnp.zeros((CAP_MAX,), jnp.int32).at[slot_place].set(flat_rows, mode="drop")
        slot_gates = jnp.zeros((CAP_MAX,), jnp.float32).at[slot_place].set(flat_gates, mode="drop")
        picked = tokens[slot_rows]
        gate_sum = jnp.dot(picked, w_gate, preferred_element_type=jnp.float32)
        up_sum = jnp.dot(picked, w_up, preferred_element_type=jnp.float32)
        hidden = (jax.nn.silu(gate_sum) * up_sum).astype(jnp.bfloat16)
        result = jnp.dot(hidden, w_down, preferred_element_type=jnp.float32).astype(jnp.bfloat16)
        running = running.at[slot_rows].add(result.astype(jnp.float32) * slot_gates[:, None])
        return running, None

    running, unused = lax.scan(one_expert, jnp.zeros((TOKENS, D), jnp.float32),
                               (experts, limits, gate_weight, up_weight, down_weight))
    return (running.astype(jnp.bfloat16), gate_weight[partner], up_weight[partner], down_weight[partner])
```

```python
import functools

import jax
import jax.numpy as jnp
from jax import lax
from jax.experimental import pallas as pl
from jax.experimental.pallas import tpu as pltpu
from jax.sharding import PartitionSpec as P

MOST = 64
CAP = 640
N = 16
MESH = pl.DeviceIdType.MESH
F32 = jnp.float32
BF16 = jnp.bfloat16
I32 = jnp.int32


def iota(shape, axis):
    return lax.broadcasted_iota(I32, shape, axis)


def rcopy(src, dst, send, recv, dev):
    return pltpu.make_async_remote_copy(
        src_ref=src, dst_ref=dst, send_sem=send, recv_sem=recv, device_id=dev, device_id_type=MESH
    )


def kernel(
    ids, gates, lim, partner, tok_h, wg_h, wu_h, wd_h,
    mixed, pg, pu, pd,
    tok, wg, wu, wd, key, gat, whi, wlo,
    xs, xr, cs, cr, offs, pm, picked,
    cbs, cbr, acc, y1s, y1r, y2s, y2r, zs, zr, hid, eo, rs, rr,
    w1g, w1u, w1d, w2g, w2u, w2d,
    loc, loc1, loc2, w1ss, w1rs, w2ss, w2rs, xss, xrs, css, crs, rss, rrs, dss, drs,
):
    tokens, width = tok_h.shape
    me = lax.axis_index("expert")
    dp = lax.axis_index("dp")
    yy, zl, cc = lax.div(dp, 4), lax.rem(lax.div(dp, 2), 2), lax.rem(dp, 2)

    def at_y(v):
        return v * 4 + zl * 2 + cc

    ya = yy + 1 - 2 * lax.rem(yy, 2)
    yb = 3 - yy
    yc = lax.rem(yy + 2, 4)
    dev_c = {"dp": dp + 1 - 2 * cc}
    dev_z = {"dp": dp + 2 - 4 * zl}
    dev_ya = {"dp": at_y(ya)}
    dev_yb = {"dp": at_y(yb)}

    loads = [
        pltpu.make_async_copy(tok_h, tok, loc.at[0]),
        pltpu.make_async_copy(wg_h.at[0], wg, loc.at[1]),
        pltpu.make_async_copy(wu_h.at[0], wu, loc.at[2]),
        pltpu.make_async_copy(wd_h.at[0], wd, loc.at[3]),
    ]
    for c in loads:
        c.start()

    barrier = pltpu.get_barrier_semaphore()

    def hello(t, _):
        pl.semaphore_signal(barrier, inc=1, device_id={"expert": lax.rem(me + t, N)}, device_id_type=MESH)
        return 0

    lax.fori_loop(1, N, hello, 0)
    for d in (dev_c, dev_z, dev_ya, dev_yb):
        pl.semaphore_signal(barrier, inc=1, device_id=d, device_id_type=MESH)
    pl.semaphore_wait(barrier, N - 1 + 4)

    def cols(i, n=128):
        return pl.ds(pl.multiple_of(i * n, n), n)

    def w1(i, k, dst):
        c = cols(i)
        return (
            rcopy(wg_h.at[0, :, c], w1g.at[dst], w1ss.at[0, k], w1rs.at[0, dst], {"expert": i}),
            rcopy(wu_h.at[0, :, c], w1u.at[dst], w1ss.at[1, k], w1rs.at[1, dst], {"expert": i}),
            rcopy(wd_h.at[0, c, :], w1d.at[dst], w1ss.at[2, k], w1rs.at[2, dst], {"expert": i}),
        )

    def w1_send(t, _):
        i = lax.rem(me + t, N)
        for c in w1(i, t, me):
            c.start()
        return 0

    lax.fori_loop(1, N, w1_send, 0)
    mine = cols(me)
    w1_local = (
        pltpu.make_async_copy(wg_h.at[0, :, mine], w1g.at[me], loc1.at[0]),
        pltpu.make_async_copy(wu_h.at[0, :, mine], w1u.at[me], loc1.at[1]),
        pltpu.make_async_copy(wd_h.at[0, mine, :], w1d.at[me], loc1.at[2]),
    )
    for c in w1_local:
        c.start()

    e_of = iota((N, tokens), 0)
    named = jnp.zeros((N, tokens), I32)
    gate = jnp.zeros((N, tokens), F32)
    for j in range(ids.shape[0]):
        eq = ids[j : j + 1, :] == e_of
        named = jnp.where(eq, 1, named)
        gate = jnp.where(eq, gates[j : j + 1, :], gate)
    run = named
    lane = iota((N, tokens), 1)
    step = 1
    while step < tokens:
        run = run + jnp.where(lane >= step, pltpu.roll(run, step, 1), 0)
        step *= 2
    key[...] = jnp.where(named > 0, run - 1, -1)
    gat[...] = gate

    loads[0].wait()
    row_of = iota((MOST, tokens), 0)

    def dispatch(t, _):
        e = lax.rem(me + t, N)
        krow = key[pl.ds(e, 1), :]
        pick = (row_of == krow).astype(F32).astype(BF16)
        rows = jnp.dot(pick, tok[...], preferred_element_type=F32).astype(BF16)
        total = jnp.sum(jnp.where(krow >= 0, 1.0, 0.0), axis=1, keepdims=True)
        total = jnp.broadcast_to(total, (8, 128))

        @pl.when(t > 0)
        def _():
            xs[e] = rows
            cs[e] = total
            rcopy(cs.at[e], cr.at[me], css.at[t], crs.at[me], {"expert": e}).start()
            rcopy(xs.at[e], xr.at[me], xss.at[t], xrs.at[me], {"expert": e}).start()

        @pl.when(t == 0)
        def _():
            xr[e] = rows
            cr[e] = total

        return 0

    lax.fori_loop(0, N, dispatch, 0)

    def spread(e, _):
        krow = key[pl.ds(e, 1), :]
        full = jnp.where(row_of == krow, gat[pl.ds(e, 1), :], 0.0)
        hi = full.astype(BF16)
        at = pl.ds(pl.multiple_of(e * MOST, MOST), MOST)
        whi[at, :] = hi
        wlo[at, :] = (full - hi.astype(F32)).astype(BF16)
        return 0

    lax.fori_loop(0, N, spread, 0)

    def x_wait(t, _):
        b = lax.rem(me + t, N)
        rcopy(cs.at[b], cr.at[b], css.at[t], crs.at[b], {"expert": b}).wait_recv()
        rcopy(xs.at[b], xr.at[b], xss.at[t], xrs.at[b], {"expert": b}).wait_recv()
        return 0

    lax.fori_loop(1, N, x_wait, 0)

    limit = lim[0:1, 0:1]
    p_of = iota((CAP, 2 * MOST), 0).astype(F32)
    l_of = iota((CAP, 2 * MOST), 1)
    i_of = lax.rem(l_of, MOST).astype(F32)

    def place(q, off):
        c0, c1 = cr[2 * q][0:1, 0:1], cr[2 * q + 1][0:1, 0:1]
        offs[2 * q] = jnp.broadcast_to(off, (8, 128))
        offs[2 * q + 1] = jnp.broadcast_to(off + c0, (8, 128))
        count = jnp.where(l_of < MOST, c0, c1)
        start = jnp.where(l_of < MOST, off, off + c0)
        hit = (p_of == start + i_of) & (i_of < count) & (p_of < limit)
        pm[:, cols(q)] = jnp.where(hit, 1.0, 0.0).astype(BF16)
        return off + c0 + c1

    lax.fori_loop(0, N // 2, place, jnp.zeros((1, 1), F32))
    picked[...] = jnp.dot(
        pm[...], xr[...].reshape(N * MOST, width), preferred_element_type=F32
    ).astype(BF16)

    half = wg.shape[1] // 2
    loads[1].wait()
    loads[2].wait()

    def theirs(j, _):
        for w, ref in enumerate((wg, wu)):
            at = pl.ds(pl.multiple_of((1 - cc) * half + j * 256, 256), 256)
            cbs[w, :, cols(j, 256)] = jnp.dot(
                picked[...], ref[:, at], preferred_element_type=F32
            ).astype(BF16)
        return 0

    def ours(j, _):
        for w, ref in enumerate((wg, wu)):
            at = pl.ds(pl.multiple_of(cc * half + j * 256, 256), 256)
            acc[w, :, cols(j, 256)] = jnp.dot(picked[...], ref[:, at], preferred_element_type=F32)
        return 0

    lax.fori_loop(0, half // 256, theirs, 0)
    to_c = rcopy(cbs, cbr, dss.at[0], drs.at[0], dev_c)
    to_c.start()
    lax.fori_loop(0, half // 256, ours, 0)
    to_c.wait_recv()

    def block(w, q):
        at = cols(q, 256)
        return acc[w, :, at] + cbr[w, :, at].astype(F32)

    y1 = []
    for w, (q, dev) in enumerate(((ya, dev_ya), (yb, dev_yb))):
        y1s[w, 0] = block(w, q).astype(BF16)
        y1s[w, 1] = block(w, yc).astype(BF16)
        c = rcopy(y1s.at[w], y1r.at[w], dss.at[1 + w], drs.at[1 + w], dev)
        c.start()
        y1.append(c)
    y2 = []
    for w, (q, dev) in enumerate(((yb, dev_yb), (ya, dev_ya))):
        y1[w].wait_recv()
        y2s[w] = (block(w, q) + y1r[w, 1].astype(F32)).astype(BF16)
        c = rcopy(y2s.at[w], y2r.at[w], dss.at[3 + w], drs.at[3 + w], dev)
        c.start()
        y2.append(c)
    for w in range(2):
        acc[w, :, cols(yy, 256)] = block(w, yy) + y1r[w, 0].astype(F32)
    for w in range(2):
        y2[w].wait_recv()
        y2f = y2r[w].astype(F32)
        lo, hi = y2f[:, :128], y2f[:, 128:]
        away = pl.ds(pl.multiple_of(yy * 256 + (1 - zl) * 128, 128), 128)
        here = pl.ds(pl.multiple_of(yy * 256 + zl * 128, 128), 128)
        zs[w] = (acc[w, :, away] + jnp.where(zl == 0, hi, lo)).astype(BF16)
        acc[w, :, here] = acc[w, :, here] + jnp.where(zl == 0, lo, hi)
    to_z = rcopy(zs, zr, dss.at[5], drs.at[5], dev_z)
    to_z.start()
    to_z.wait_recv()
    here = pl.ds(pl.multiple_of(yy * 256 + zl * 128, 128), 128)
    gsum = acc[0, :, here] + zr[0].astype(F32)
    usum = acc[1, :, here] + zr[1].astype(F32)
    own = cols(cc * 8 + yy * 2 + zl)
    hid[:, own] = (gsum / (1.0 + jnp.exp(-gsum)) * usum).astype(BF16)

    def chunk(c, q):
        return cols(c * 4 + q, 256)

    h_z = rcopy(hid.at[:, own], hid.at[:, own], dss.at[6], drs.at[6], dev_z)
    h_z.start()
    h_z_in = cols(cc * 8 + yy * 2 + 1 - zl)
    rcopy(hid.at[:, h_z_in], hid.at[:, h_z_in], dss.at[6], drs.at[6], dev_z).wait_recv()
    me_q = chunk(cc, yy)

    def to(at, k, dev):
        return rcopy(hid.at[at[0], at[1]], hid.at[at[0], at[1]], dss.at[k], drs.at[k], dev)

    everyrow, top, low = pl.ds(0, CAP), pl.ds(0, CAP // 2), pl.ds(CAP // 2, CAP // 2)
    h_ya = to((everyrow, me_q), 7, dev_ya)
    h_yb = to((everyrow, me_q), 8, dev_yb)
    h_ya.start()
    h_yb.start()
    h_c0 = to((everyrow, me_q), 9, dev_c)
    h_c0.start()
    to((everyrow, chunk(cc, ya)), 7, dev_ya).wait_recv()
    h_fa = to((top, chunk(cc, ya)), 10, dev_yb)
    h_fa.start()
    h_c1 = to((everyrow, chunk(cc, ya)), 11, dev_c)
    h_c1.start()
    to((everyrow, chunk(cc, yb)), 8, dev_yb).wait_recv()
    h_fb = to((low, chunk(cc, yb)), 12, dev_ya)
    h_fb.start()
    h_c2 = to((everyrow, chunk(cc, yb)), 13, dev_c)
    h_c2.start()
    to((top, chunk(cc, yc)), 10, dev_yb).wait_recv()
    to((low, chunk(cc, yc)), 12, dev_ya).wait_recv()
    h_c3 = to((everyrow, chunk(cc, yc)), 14, dev_c)
    h_c3.start()
    to((everyrow, chunk(1 - cc, yy)), 9, dev_c).wait_recv()
    to((everyrow, chunk(1 - cc, ya)), 11, dev_c).wait_recv()
    to((everyrow, chunk(1 - cc, yb)), 13, dev_c).wait_recv()
    to((everyrow, chunk(1 - cc, yc)), 14, dev_c).wait_recv()

    loads[3].wait()
    eo[...] = jnp.dot(hid[...], wd[...], preferred_element_type=F32).astype(BF16)

    i_row = iota((MOST, CAP), 0).astype(F32)
    p_lane = iota((MOST, CAP), 1).astype(F32)

    def reply(t, _):
        b = lax.rem(me + t, N)
        count, start = cr[b][0:1, 0:1], offs[b][0:1, 0:1]
        hit = (p_lane == start + i_row) & (i_row < count) & (p_lane < limit)
        rows = jnp.dot(
            jnp.where(hit, 1.0, 0.0).astype(BF16), eo[...], preferred_element_type=F32
        ).astype(BF16)

        @pl.when(t > 0)
        def _():
            rs[b] = rows
            rcopy(rs.at[b], rr.at[me], rss.at[t], rrs.at[me], {"expert": b}).start()

        @pl.when(t == 0)
        def _():
            rr[b] = rows

        return 0

    lax.fori_loop(0, N, reply, 0)

    for c in w1_local:
        c.wait()

    def w1_wait(t, _):
        s = lax.rem(me + t, N)
        for c in w1(me, t, s):
            c.wait_recv()
        return 0

    lax.fori_loop(1, N, w1_wait, 0)

    def w2(k, t, i):
        c = cols(i)
        return (
            rcopy(w2g.at[k], pg.at[0, :, c], w2ss.at[0, t], w2rs.at[0, i], {"expert": k}),
            rcopy(w2u.at[k], pu.at[0, :, c], w2ss.at[1, t], w2rs.at[1, i], {"expert": k}),
            rcopy(w2d.at[k], pd.at[0, c, :], w2ss.at[2, t], w2rs.at[2, i], {"expert": k}),
        )

    def w2_send(t, _):
        k = lax.rem(me + t, N)
        s = partner[k]
        w2g[k] = w1g[s]
        w2u[k] = w1u[s]
        w2d[k] = w1d[s]

        @pl.when(t > 0)
        def _():
            for c in w2(k, t, me):
                c.start()

        return 0

    lax.fori_loop(0, N, w2_send, 0)
    w2_local = (
        pltpu.make_async_copy(w2g.at[me], pg.at[0, :, mine], loc2.at[0]),
        pltpu.make_async_copy(w2u.at[me], pu.at[0, :, mine], loc2.at[1]),
        pltpu.make_async_copy(w2d.at[me], pd.at[0, mine, :], loc2.at[2]),
    )
    for c in w2_local:
        c.start()

    def r_wait(t, _):
        b = lax.rem(me + t, N)
        rcopy(rs.at[b], rr.at[b], rss.at[t], rrs.at[b], {"expert": b}).wait_recv()
        return 0

    lax.fori_loop(1, N, r_wait, 0)

    def combine(j, _):
        at = cols(j, 256)
        back = rr[...].reshape(N * MOST, width)
        over = (((0,), (0,)), ((), ()))
        total = lax.dot_general(whi[:, at], back, over, preferred_element_type=F32)
        total = total + lax.dot_general(wlo[:, at], back, over, preferred_element_type=F32)
        mixed[at, :] = total.astype(BF16)
        return 0

    lax.fori_loop(0, tokens // 256, combine, 0)

    for c in w2_local:
        c.wait()

    def w2_wait(t, _):
        i = lax.rem(me + t, N)
        for c in w2(me, t, i):
            c.wait_recv()
        return 0

    lax.fori_loop(1, N, w2_wait, 0)

    def sent(t, _):
        i = lax.rem(me + t, N)
        for c in w1(i, t, me):
            c.wait_send()
        for c in w2(i, t, me):
            c.wait_send()
        rcopy(cs.at[i], cr.at[me], css.at[t], crs.at[me], {"expert": i}).wait_send()
        rcopy(xs.at[i], xr.at[me], xss.at[t], xrs.at[me], {"expert": i}).wait_send()
        rcopy(rs.at[i], rr.at[me], rss.at[t], rrs.at[me], {"expert": i}).wait_send()
        return 0

    lax.fori_loop(1, N, sent, 0)
    for c in (to_c, *y1, *y2, to_z, h_z, h_ya, h_yb, h_c0, h_fa, h_c1, h_fb, h_c2, h_c3):
        c.wait_send()


def local(tokens, expert_ids, gates, gate_weight, up_weight, down_weight, partner, capacity):
    rows, width = tokens.shape
    ff = gate_weight.shape[2]
    me = lax.axis_index("expert")
    slots = jnp.arange(N, dtype=I32)
    mate = jnp.sum(jnp.where(slots == me, partner, 0))
    limit = jnp.sum(jnp.where(slots == mate, capacity, 0)).astype(F32)
    lim = jnp.broadcast_to(limit, (8, 128))
    piece = ff // N
    vmem = pl.BlockSpec(memory_space=pltpu.VMEM)
    smem = pl.BlockSpec(memory_space=pltpu.SMEM)
    anyw = pl.BlockSpec(memory_space=pl.ANY)
    V, D = pltpu.VMEM, pltpu.SemaphoreType.DMA
    return pl.pallas_call(
        kernel,
        out_shape=(
            jax.ShapeDtypeStruct((rows, width), BF16),
            jax.ShapeDtypeStruct(gate_weight.shape, BF16),
            jax.ShapeDtypeStruct(up_weight.shape, BF16),
            jax.ShapeDtypeStruct(down_weight.shape, BF16),
        ),
        in_specs=[vmem, vmem, vmem, smem, anyw, anyw, anyw, anyw],
        out_specs=(vmem, anyw, anyw, anyw),
        scratch_shapes=[
            V((rows, width), BF16), V((width, ff), BF16), V((width, ff), BF16), V((ff, width), BF16),
            V((N, rows), I32), V((N, rows), F32), V((N * MOST, rows), BF16), V((N * MOST, rows), BF16),
            V((N, MOST, width), BF16), V((N, MOST, width), BF16), V((N, 8, 128), F32), V((N, 8, 128), F32),
            V((N, 8, 128), F32), V((CAP, N * MOST), BF16), V((CAP, width), BF16),
            V((2, CAP, ff // 2), BF16), V((2, CAP, ff // 2), BF16), V((2, CAP, ff // 2), F32),
            V((2, 2, CAP, 256), BF16), V((2, 2, CAP, 256), BF16), V((2, CAP, 256), BF16), V((2, CAP, 256), BF16),
            V((2, CAP, 128), BF16), V((2, CAP, 128), BF16), V((CAP, ff), BF16), V((CAP, width), BF16),
            V((N, MOST, width), BF16), V((N, MOST, width), BF16),
            V((N, width, piece), BF16), V((N, width, piece), BF16), V((N, piece, width), BF16),
            V((N, width, piece), BF16), V((N, width, piece), BF16), V((N, piece, width), BF16),
            D((4,)), D((3,)), D((3,)), D((3, N)), D((3, N)), D((3, N)), D((3, N)),
            D((N,)), D((N,)), D((N,)), D((N,)), D((N,)), D((N,)), D((16,)), D((16,)),
        ],
        compiler_params=pltpu.CompilerParams(
            collective_id=0, has_side_effects=True, vmem_limit_bytes=67043328
        ),
        name="moe_swap",
    )(expert_ids.T, gates.T, lim, partner, tokens, gate_weight, up_weight, down_weight)


def solution(mesh):
    return jax.shard_map(
        local,
        mesh=mesh,
        in_specs=(
            P("expert", "dp"),
            P("expert", None),
            P("expert", None),
            P("expert", "dp", None),
            P("expert", "dp", None),
            P("expert", None, "dp"),
            P(),
            P(),
        ),
        out_specs=(
            P("expert", "dp"),
            P("expert", "dp", None),
            P("expert", "dp", None),
            P("expert", None, "dp"),
        ),
        check_vma=False,
    )
```

```python
import functools

import jax
import jax.numpy as jnp
from jax import lax
from jax.experimental import pallas as pl
from jax.experimental.pallas import tpu as pltpu
from jax.sharding import PartitionSpec as P

MOST = 64
CAP = 640
N = 16
MESH = pl.DeviceIdType.MESH
F32 = jnp.float32
BF16 = jnp.bfloat16
I32 = jnp.int32
LANES = (((1,), (1,)), ((), ()))
ROWS = (((0,), (0,)), ((), ()))
EARLY = 4


def iota(shape, axis):
    return lax.broadcasted_iota(I32, shape, axis)


def rcopy(src, dst, send, recv, dev):
    return pltpu.make_async_remote_copy(
        src_ref=src, dst_ref=dst, send_sem=send, recv_sem=recv, device_id=dev, device_id_type=MESH
    )


def kernel(
    ids, gates, capacity, partner, tok_h, wg_h, wu_h, wd_h,
    mixed, pg, pu, pd,
    tok, wg, wu, wd, key, gat, whi, wlo,
    xs, xr, cs, cr, offs, pm, picked,
    cbs, cbr, acc, y1s, y1r, y2s, y2r, zs, zr, hid, eo, rs, rr,
    w1b, w2b,
    loc, w1ss, w1rs, w2ss, w2rs, xss, xrs, css, crs, rss, rrs, dss, drs,
):
    width, tokens = tok_h.shape
    me = lax.axis_index("expert")
    dp = lax.axis_index("dp")
    yy, zl, cc = lax.div(dp, 4), lax.rem(lax.div(dp, 2), 2), lax.rem(dp, 2)

    def at_y(v):
        return v * 4 + zl * 2 + cc

    ya = yy + 1 - 2 * lax.rem(yy, 2)
    yb = 3 - yy
    yc = lax.rem(yy + 2, 4)
    dev_c = {"dp": dp + 1 - 2 * cc}
    dpz = dp + 2 - 4 * zl
    dev_z = {"dp": dpz}
    dev_ya = {"dp": at_y(ya)}
    dev_yb = {"dp": at_y(yb)}

    loads = [
        pltpu.make_async_copy(tok_h, tok, loc.at[0]),
        pltpu.make_async_copy(wg_h.at[0], wg, loc.at[1]),
        pltpu.make_async_copy(wu_h.at[0], wu, loc.at[2]),
        pltpu.make_async_copy(wd_h.at[0], wd, loc.at[3]),
    ]
    for c in loads:
        c.start()

    barrier = pltpu.get_barrier_semaphore()

    def hello(t, _):
        pl.semaphore_signal(barrier, inc=1, device_id={"expert": lax.rem(me + t, N)}, device_id_type=MESH)
        return 0

    def hello_z(t, _):
        dev = {"dp": dpz, "expert": lax.rem(me + t, N)}
        pl.semaphore_signal(barrier, inc=1, device_id=dev, device_id_type=MESH)
        return 0

    lax.fori_loop(1, N, hello, 0)
    lax.fori_loop(0, N, hello_z, 0)
    for d in (dev_c, dev_ya, dev_yb):
        pl.semaphore_signal(barrier, inc=1, device_id=d, device_id_type=MESH)
    pl.semaphore_wait(barrier, 2 * N - 1 + 3)

    def turn(t):
        return lax.rem(me + 5 * t, N)

    def cols(i, n=128):
        return pl.ds(pl.multiple_of(i * n, n), n)

    e_of = iota((N, tokens), 0)
    named = jnp.zeros((N, tokens), I32)
    gate = jnp.zeros((N, tokens), F32)
    for j in range(ids.shape[0]):
        eq = ids[j : j + 1, :] == e_of
        named = jnp.where(eq, 1, named)
        gate = jnp.where(eq, gates[j : j + 1, :], gate)
    run = named
    lane = iota((N, tokens), 1)
    step = 1
    while step < tokens:
        run = run + jnp.where(lane >= step, pltpu.roll(run, step, 1), 0)
        step *= 2
    key[...] = jnp.where(named > 0, run - 1, -1)
    gat[...] = gate

    loads[0].wait()
    row_of = iota((MOST, tokens), 0)

    def dispatch(t, _):
        e = turn(t)
        krow = key[pl.ds(e, 1), :]
        pick = (row_of == krow).astype(F32).astype(BF16)
        rows = lax.dot_general(pick, tok[...], LANES, preferred_element_type=F32).astype(BF16)
        total = jnp.sum(jnp.where(krow >= 0, 1.0, 0.0), axis=1, keepdims=True)
        total = jnp.broadcast_to(total, (8, 128))

        @pl.when(t > 0)
        def _():
            xs[e] = rows
            cs[e] = total
            rcopy(cs.at[e], cr.at[me], css.at[t], crs.at[me], {"expert": e}).start()
            rcopy(xs.at[e], xr.at[me], xss.at[t], xrs.at[me], {"expert": e}).start()

        @pl.when(t == 0)
        def _():
            xr[e] = rows
            cr[e] = total

        return 0

    lax.fori_loop(0, N, dispatch, 0)

    def w1(i, t, src):
        return [
            rcopy(ref.at[0, :, cols(i)], w1b.at[n, src], w1ss.at[n, t], w1rs.at[n, src], {"dp": dpz, "expert": i})
            for n, ref in enumerate((wg_h, wu_h, wd_h))
        ]

    def w1_send(t, _):
        for c in w1(turn(t), t, me):
            c.start()
        return 0

    lax.fori_loop(0, N, w1_send, 0)

    def spread(e, _):
        krow = key[pl.ds(e, 1), :]
        full = jnp.where(row_of == krow, gat[pl.ds(e, 1), :], 0.0)
        hi = full.astype(BF16)
        at = pl.ds(pl.multiple_of(e * MOST, MOST), MOST)
        whi[at, :] = hi
        wlo[at, :] = (full - hi.astype(F32)).astype(BF16)
        return 0

    lax.fori_loop(0, N, spread, 0)

    def x_wait(t, _):
        b = turn(t)
        rcopy(cs.at[b], cr.at[b], css.at[t], crs.at[b], {"expert": b}).wait_recv()
        rcopy(xs.at[b], xr.at[b], xss.at[t], xrs.at[b], {"expert": b}).wait_recv()
        return 0

    lax.fori_loop(1, N, x_wait, 0)

    limit = capacity[partner[me]].astype(F32)
    p_of = iota((CAP, 2 * MOST), 0).astype(F32)
    l_of = iota((CAP, 2 * MOST), 1)
    i_of = lax.rem(l_of, MOST).astype(F32)

    def place(q, off):
        c0, c1 = cr[2 * q][0:1, 0:1], cr[2 * q + 1][0:1, 0:1]
        offs[2 * q] = jnp.broadcast_to(off, (8, 128))
        offs[2 * q + 1] = jnp.broadcast_to(off + c0, (8, 128))
        count = jnp.where(l_of < MOST, c0, c1)
        start = jnp.where(l_of < MOST, off, off + c0)
        hit = (p_of == start + i_of) & (i_of < count) & (p_of < limit)
        pm[:, cols(q)] = jnp.where(hit, 1.0, 0.0).astype(BF16)
        return off + c0 + c1

    lax.fori_loop(0, N // 2, place, jnp.zeros((1, 1), F32))
    picked[...] = jnp.dot(
        pm[...], xr[...].reshape(N * MOST, width), preferred_element_type=F32
    ).astype(BF16)

    half = wg.shape[1] // 2
    loads[1].wait()
    loads[2].wait()

    def theirs(j, _):
        for w, ref in enumerate((wg, wu)):
            at = pl.ds(pl.multiple_of((1 - cc) * half + j * 256, 256), 256)
            cbs[w, :, cols(j, 256)] = jnp.dot(picked[...], ref[:, at], preferred_element_type=F32)
        return 0

    def ours(j, _):
        for w, ref in enumerate((wg, wu)):
            at = pl.ds(pl.multiple_of(cc * half + j * 256, 256), 256)
            acc[w, :, cols(j, 256)] = jnp.dot(picked[...], ref[:, at], preferred_element_type=F32)
        return 0

    lax.fori_loop(0, half // 256, theirs, 0)
    to_c = rcopy(cbs, cbr, dss.at[0], drs.at[0], dev_c)
    to_c.start()
    lax.fori_loop(0, half // 256, ours, 0)
    to_c.wait_recv()

    def block(w, q):
        at = cols(q, 256)
        return acc[w, :, at] + cbr[w, :, at]

    y1 = []
    for w, (q, dev) in enumerate(((ya, dev_ya), (yb, dev_yb))):
        y1s[w, 0] = block(w, q).astype(BF16)
        y1s[w, 1] = block(w, yc).astype(BF16)
        c = rcopy(y1s.at[w], y1r.at[w], dss.at[1 + w], drs.at[1 + w], dev)
        c.start()
        y1.append(c)
    y2 = []
    for w, (q, dev) in enumerate(((yb, dev_yb), (ya, dev_ya))):
        y1[w].wait_recv()
        y2s[w] = (block(w, q) + y1r[w, 1].astype(F32)).astype(BF16)
        c = rcopy(y2s.at[w], y2r.at[w], dss.at[3 + w], drs.at[3 + w], dev)
        c.start()
        y2.append(c)
    for w in range(2):
        acc[w, :, cols(yy, 256)] = block(w, yy) + y1r[w, 0].astype(F32)
    for w in range(2):
        y2[w].wait_recv()
        y2f = y2r[w].astype(F32)
        lo, hi = y2f[:, :128], y2f[:, 128:]
        away = pl.ds(pl.multiple_of(yy * 256 + (1 - zl) * 128, 128), 128)
        here = pl.ds(pl.multiple_of(yy * 256 + zl * 128, 128), 128)
        zs[w] = (acc[w, :, away] + jnp.where(zl == 0, hi, lo)).astype(BF16)
        acc[w, :, here] = acc[w, :, here] + jnp.where(zl == 0, lo, hi)
    to_z = rcopy(zs, zr, dss.at[5], drs.at[5], dev_z)
    to_z.start()
    to_z.wait_recv()
    here = pl.ds(pl.multiple_of(yy * 256 + zl * 128, 128), 128)
    gsum = acc[0, :, here] + zr[0].astype(F32)
    usum = acc[1, :, here] + zr[1].astype(F32)
    own = cols(cc * 8 + yy * 2 + zl)
    hid[:, own] = (gsum / (1.0 + jnp.exp(-gsum)) * usum).astype(BF16)

    def chunk(c, q):
        return cols(c * 4 + q, 256)

    h_z = rcopy(hid.at[:, own], hid.at[:, own], dss.at[6], drs.at[6], dev_z)
    h_z.start()
    h_z_in = cols(cc * 8 + yy * 2 + 1 - zl)
    rcopy(hid.at[:, h_z_in], hid.at[:, h_z_in], dss.at[6], drs.at[6], dev_z).wait_recv()
    me_q = chunk(cc, yy)

    def to(at, k, dev):
        return rcopy(hid.at[at[0], at[1]], hid.at[at[0], at[1]], dss.at[k], drs.at[k], dev)

    everyrow, top, low = pl.ds(0, CAP), pl.ds(0, CAP // 2), pl.ds(CAP // 2, CAP // 2)
    h_ya = to((everyrow, me_q), 7, dev_ya)
    h_yb = to((everyrow, me_q), 8, dev_yb)
    h_ya.start()
    h_yb.start()
    h_c0 = to((everyrow, me_q), 9, dev_c)
    h_c0.start()
    def w1_wait(t, _):
        for c in w1(me, t, turn(t)):
            c.wait_recv()
        return 0

    def w2(k, t, src):
        return [
            rcopy(w2b.at[n, k], ref.at[0, :, cols(src)], w2ss.at[n, t], w2rs.at[n, src], {"dp": dpz, "expert": k})
            for n, ref in enumerate((pg, pu, pd))
        ]

    def w2_send(t, _):
        k = turn(t)
        s = partner[k]
        for n in range(3):
            w2b[n, k] = w1b[n, s]
        for c in w2(k, t, me):
            c.start()
        return 0

    lax.fori_loop(0, N, w1_wait, 0)
    lax.fori_loop(0, EARLY, w2_send, 0)

    to((everyrow, chunk(cc, ya)), 7, dev_ya).wait_recv()
    h_fa = to((top, chunk(cc, ya)), 10, dev_yb)
    h_fa.start()
    h_c1 = to((everyrow, chunk(cc, ya)), 11, dev_c)
    h_c1.start()
    to((everyrow, chunk(cc, yb)), 8, dev_yb).wait_recv()
    h_fb = to((low, chunk(cc, yb)), 12, dev_ya)
    h_fb.start()
    h_c2 = to((everyrow, chunk(cc, yb)), 13, dev_c)
    h_c2.start()
    to((top, chunk(cc, yc)), 10, dev_yb).wait_recv()
    to((low, chunk(cc, yc)), 12, dev_ya).wait_recv()
    h_c3 = to((everyrow, chunk(cc, yc)), 14, dev_c)
    h_c3.start()
    to((everyrow, chunk(1 - cc, yy)), 9, dev_c).wait_recv()
    to((everyrow, chunk(1 - cc, ya)), 11, dev_c).wait_recv()
    to((everyrow, chunk(1 - cc, yb)), 13, dev_c).wait_recv()
    to((everyrow, chunk(1 - cc, yc)), 14, dev_c).wait_recv()

    loads[3].wait()
    eo[...] = lax.dot_general(hid[...], wd[...], LANES, preferred_element_type=F32).astype(BF16)

    i_row = iota((MOST, CAP), 0).astype(F32)
    p_lane = iota((MOST, CAP), 1).astype(F32)

    def reply(t, _):
        b = turn(t)
        count, start = cr[b][0:1, 0:1], offs[b][0:1, 0:1]
        hit = (p_lane == start + i_row) & (i_row < count) & (p_lane < limit)
        rows = jnp.dot(
            jnp.where(hit, 1.0, 0.0).astype(BF16), eo[...], preferred_element_type=F32
        ).astype(BF16)

        @pl.when(t > 0)
        def _():
            rs[b] = rows
            rcopy(rs.at[b], rr.at[me], rss.at[t], rrs.at[me], {"expert": b}).start()

        @pl.when(t == 0)
        def _():
            rr[b] = rows

        return 0

    lax.fori_loop(0, N, reply, 0)

    lax.fori_loop(EARLY, N, w2_send, 0)

    def r_wait(t, _):
        b = turn(t)
        rcopy(rs.at[b], rr.at[b], rss.at[t], rrs.at[b], {"expert": b}).wait_recv()
        return 0

    lax.fori_loop(1, N, r_wait, 0)

    def combine(j, _):
        at = cols(j, 256)
        back = rr[...].reshape(N * MOST, width)
        total = lax.dot_general(back, whi[:, at], ROWS, preferred_element_type=F32)
        total = total + lax.dot_general(back, wlo[:, at], ROWS, preferred_element_type=F32)
        mixed[:, at] = total.astype(BF16)
        return 0

    lax.fori_loop(0, tokens // 256, combine, 0)

    def w2_wait(t, _):
        for c in w2(me, t, turn(t)):
            c.wait_recv()
        return 0

    lax.fori_loop(0, N, w2_wait, 0)

    def w_sent(t, _):
        for c in w1(turn(t), t, me):
            c.wait_send()
        for c in w2(turn(t), t, me):
            c.wait_send()
        return 0

    lax.fori_loop(0, N, w_sent, 0)

    def sent(t, _):
        i = turn(t)
        rcopy(cs.at[i], cr.at[me], css.at[t], crs.at[me], {"expert": i}).wait_send()
        rcopy(xs.at[i], xr.at[me], xss.at[t], xrs.at[me], {"expert": i}).wait_send()
        rcopy(rs.at[i], rr.at[me], rss.at[t], rrs.at[me], {"expert": i}).wait_send()
        return 0

    lax.fori_loop(1, N, sent, 0)
    for c in (to_c, *y1, *y2, to_z, h_z, h_ya, h_yb, h_c0, h_fa, h_c1, h_fb, h_c2, h_c3):
        c.wait_send()


def local(tokens, expert_ids, gates, gate_weight, up_weight, down_weight, partner, capacity):
    rows, width = tokens.shape
    ff = gate_weight.shape[2]
    vmem = pl.BlockSpec(memory_space=pltpu.VMEM)
    smem = pl.BlockSpec(memory_space=pltpu.SMEM)
    anyw = pl.BlockSpec(memory_space=pl.ANY)
    V, D = pltpu.VMEM, pltpu.SemaphoreType.DMA
    mix, new_gate, new_up, new_down = pl.pallas_call(
        kernel,
        out_shape=(
            jax.ShapeDtypeStruct((width, rows), BF16),
            jax.ShapeDtypeStruct(gate_weight.shape, BF16),
            jax.ShapeDtypeStruct(up_weight.shape, BF16),
            jax.ShapeDtypeStruct(gate_weight.shape, BF16),
        ),
        in_specs=[vmem, vmem, smem, smem, anyw, anyw, anyw, anyw],
        out_specs=(vmem, anyw, anyw, anyw),
        scratch_shapes=[
            V((width, rows), BF16), V((width, ff), BF16), V((width, ff), BF16), V((width, ff), BF16),
            V((N, rows), I32), V((N, rows), F32), V((N * MOST, rows), BF16), V((N * MOST, rows), BF16),
            V((N, MOST, width), BF16), V((N, MOST, width), BF16), V((N, 8, 128), F32), V((N, 8, 128), F32),
            V((N, 8, 128), F32), V((CAP, N * MOST), BF16), V((CAP, width), BF16),
            V((2, CAP, ff // 2), F32), V((2, CAP, ff // 2), F32), V((2, CAP, ff // 2), F32),
            V((2, 2, CAP, 256), BF16), V((2, 2, CAP, 256), BF16), V((2, CAP, 256), BF16), V((2, CAP, 256), BF16),
            V((2, CAP, 128), BF16), V((2, CAP, 128), BF16), V((CAP, ff), BF16), V((CAP, width), BF16),
            V((N, MOST, width), BF16), V((N, MOST, width), BF16),
            V((3, N, width, ff // N), BF16), V((3, N, width, ff // N), BF16),
            D((4,)), D((3, N)), D((3, N)), D((3, N)), D((3, N)),
            D((N,)), D((N,)), D((N,)), D((N,)), D((N,)), D((N,)), D((16,)), D((16,)),
        ],
        compiler_params=pltpu.CompilerParams(
            collective_id=0, has_side_effects=True, vmem_limit_bytes=67043328
        ),
        name="moe_swap",
    )(expert_ids.T, gates.T, capacity, partner, tokens.T, gate_weight, up_weight, down_weight.transpose(0, 2, 1))
    return mix.T, new_gate, new_up, new_down.transpose(0, 2, 1)


def solution(mesh):
    return jax.shard_map(
        local,
        mesh=mesh,
        in_specs=(
            P("expert", "dp"),
            P("expert", None),
            P("expert", None),
            P("expert", "dp", None),
            P("expert", "dp", None),
            P("expert", None, "dp"),
            P(),
            P(),
        ),
        out_specs=(
            P("expert", "dp"),
            P("expert", "dp", None),
            P("expert", "dp", None),
            P("expert", None, "dp"),
        ),
        check_vma=False,
    )
```

```python
import functools

import jax
import jax.numpy as jnp
from jax import lax
from jax.experimental import pallas as pl
from jax.experimental.pallas import tpu as pltpu
from jax.sharding import PartitionSpec as P

MOST = 64
CAP = 640
N = 16
MESH = pl.DeviceIdType.MESH
F32 = jnp.float32
BF16 = jnp.bfloat16
I32 = jnp.int32
LANES = (((1,), (1,)), ((), ()))
ROWS = (((0,), (0,)), ((), ()))
EARLY = 4
SWAP_REFS = {True: 6, False: 13}
PLANS = ((1, 1), None)


def iota(shape, axis):
    return lax.broadcasted_iota(I32, shape, axis)


def rcopy(src, dst, send, recv, dev):
    return pltpu.make_async_remote_copy(
        src_ref=src, dst_ref=dst, send_sem=send, recv_sem=recv, device_id=dev, device_id_type=MESH
    )


def spread_swap(me, dpz, cols, turn, partner, weights, placed, w1b, w2b, w1ss, w1rs, w2ss, w2rs):
    def w1(i, t, src):
        return [
            rcopy(ref.at[0, :, cols(i)], w1b.at[n, src], w1ss.at[n, t], w1rs.at[n, src], {"dp": dpz, "expert": i})
            for n, ref in enumerate(weights)
        ]

    def w2(k, t, src):
        return [
            rcopy(w2b.at[n, k], ref.at[0, :, cols(src)], w2ss.at[n, t], w2rs.at[n, src], {"dp": dpz, "expert": k})
            for n, ref in enumerate(placed)
        ]

    def w1_send(t, _):
        for c in w1(turn(t), t, me):
            c.start()
        return 0

    def w1_wait(t, _):
        for c in w1(me, t, turn(t)):
            c.wait_recv()
        return 0

    def w2_send(t, _):
        k = turn(t)
        s = partner[k]
        for n in range(3):
            w2b[n, k] = w1b[n, s]
        for c in w2(k, t, me):
            c.start()
        return 0

    def w2_wait(t, _):
        for c in w2(me, t, turn(t)):
            c.wait_recv()
        return 0

    def w_sent(t, _):
        for c in w1(turn(t), t, me) + w2(turn(t), t, me):
            c.wait_send()
        return 0

    def swap(point):
        if point == 1:
            lax.fori_loop(0, N, w1_send, 0)
        if point == 6:
            lax.fori_loop(0, N, w1_wait, 0)
            lax.fori_loop(0, EARLY, w2_send, 0)
        if point == 8:
            lax.fori_loop(EARLY, N, w2_send, 0)
        if point == 9:
            lax.fori_loop(0, N, w2_wait, 0)
            lax.fori_loop(0, N, w_sent, 0)

    return swap


def row_swap(
    plan, me, partner, weights, placed, q0, q1, q2, e0, e1, e2, zsend, relay, xsend, xrelay, local_sem, ss, rs
):
    near, far = plan
    row_box, far_box = (q0, q1, q2), (e0, e1, e2)
    r, x = lax.div(me, 4), lax.rem(me, 4)
    rp, rm = lax.rem(r + 1, 4), lax.rem(r + 3, 4)
    xp, xm, xo = lax.rem(x + 1, 4), lax.rem(x + 3, 4), lax.rem(x + 2, 4)
    quarter = q0.shape[2]
    left, right = pl.ds(0, quarter // 2), pl.ds(quarter // 2, quarter // 2)
    opposite = 2 * near

    def at(row, col):
        return {"expert": row * 4 + col}

    def part(ref, j):
        return ref.at[0, :, pl.ds(pl.multiple_of(j * quarter, quarter), quarter)]

    def row_at(i):
        return lax.div(partner[i], 4)

    def find(target, k):
        seen, found = 0, 0
        for i in range(4):
            hit = row_at(r * 4 + i) == target
            found = jnp.where(hit & (seen == k), i, found)
            seen = seen + jnp.where(hit, 1, 0)
        return found

    def held(col):
        s = partner[r * 4 + col]
        sr, si = lax.div(s, 4), lax.rem(s, 4)
        order = 0
        for i in range(4):
            order = order + jnp.where((si > i) & (row_at(sr * 4 + i) == r), 1, 0)
        d = lax.rem(sr - r + 4, 4)
        place = jnp.where(d == 3, order, jnp.where(d == 1, near + order, opposite + order))
        return d == 0, si, jnp.minimum(place, e0.shape[0] - 1)

    def x1(n, sender=False):
        ways = ((xp, xm), (xm, xp), (xo, xo))
        return [
            rcopy(part(weights[n], to), row_box[n].at[x if sender else src], ss.at[n, d], rs.at[n, d], at(r, to))
            for d, (to, src) in enumerate(ways)
        ]

    def x1_local(n):
        return pltpu.make_async_copy(part(weights[n], x), row_box[n].at[x], local_sem.at[n])

    def z1(n, group):
        out = []
        if group:
            for k in range(near):
                out.append((zsend.at[n, k], far_box[n].at[k], rp))
                out.append((zsend.at[n, near + k], far_box[n].at[near + k], rm))
        else:
            for k in range(far):
                out.append((zsend.at[n, 2 * near + k, :, left], relay.at[n, 0, k], rp))
                out.append((zsend.at[n, 2 * near + k, :, right], relay.at[n, 1, k], rm))
        first = 3 + 2 * far * group
        return [
            rcopy(a, b, ss.at[n, first + i], rs.at[n, first + i], at(row, x)) for i, (a, b, row) in enumerate(out)
        ]

    def z2(n):
        out = []
        for k in range(far):
            for w, (cut, row) in enumerate(((left, rp), (right, rm))):
                i = 16 + 2 * k + w
                out.append(
                    rcopy(relay.at[n, w, k], far_box[n].at[opposite + k, :, cut], ss.at[n, i], rs.at[n, i], at(row, x))
                )
        return out

    def x2(n, sender=False):
        return [
            rcopy(xsend.at[n, 1], part(placed[n], x if sender else xm), ss.at[n, 26], rs.at[n, 26], at(r, xp)),
            rcopy(xsend.at[n, 2], part(placed[n], x if sender else xp), ss.at[n, 27], rs.at[n, 27], at(r, xm)),
        ]

    def x2_first(n):
        return rcopy(xsend.at[n, 3], xrelay.at[n], ss.at[n, 28], rs.at[n, 28], at(r, xm))

    def x2_last(n, sender=False):
        return rcopy(
            xrelay.at[n], part(placed[n], xp if sender else xo), ss.at[n, 29], rs.at[n, 29], at(r, xm)
        )

    def x2_local(n):
        return pltpu.make_async_copy(xsend.at[n, 0], part(placed[n], x), local_sem.at[3 + n])

    def x1_send(n):
        for c in x1(n, True):
            c.start()
        x1_local(n).start()

    def z1_send(n):
        for c in x1(n):
            c.wait_recv()
        x1_local(n).wait()
        for k in range(far):
            zsend[n, 2 * near + k] = row_box[n][find(lax.rem(r + 2, 4), k)]
        for k in range(near):
            zsend[n, k] = row_box[n][find(rp, k)]
            zsend[n, near + k] = row_box[n][find(rm, k)]
        for c in z1(n, 0) + z1(n, 1):
            c.start()

    def z2_send(n):
        for c in z1(n, 0):
            c.wait_recv()
        for c in z2(n):
            c.start()

    def x2_send(n):
        for c in z1(n, 1) + z2(n):
            c.wait_recv()
        for j, col in enumerate((x, xp, xm, xo)):
            stays, si, place = held(col)
            xsend[n, j] = jnp.where(stays, row_box[n][si], far_box[n][place])
        for c in [x2_first(n)] + x2(n, True):
            c.start()
        x2_local(n).start()

    def x2_relay(n):
        x2_first(n).wait_recv()
        x2_last(n, True).start()

    def finish(n):
        for c in x2(n):
            c.wait_recv()
        x2_last(n).wait_recv()
        x2_local(n).wait()
        for c in x1(n, True) + z1(n, 0) + z1(n, 1) + z2(n) + x2(n, True) + [x2_first(n), x2_last(n, True)]:
            c.wait_send()

    def swap(point):
        if point == 0:
            x1_send(0)
        if point == 1:
            x1_send(1)
            x1_send(2)
        if point == 2:
            z1_send(0)
        if point == 3:
            z1_send(1)
        if point == 6:
            z2_send(0)
            z1_send(2)
            z2_send(1)
        if point == 8:
            x2_send(0)
            z2_send(2)
            x2_send(1)
            x2_relay(0)
        if point == 9:
            x2_send(2)
            for n in range(1, 3):
                x2_relay(n)
            for n in range(3):
                finish(n)

    return swap


def kernel(plan, *refs):
    (
        ids, gates, capacity, partner, tok_h, wg_h, wu_h, wd_h,
        mixed, pg, pu, pd,
        tok, wg, wu, wd, key, gat, whi, wlo,
        xs, xr, cs, cr, offs, pm, picked,
        cbs, cbr, acc, y1s, y1r, y2s, y2r, zs, zr, hid, eo, rs, rr,
        loc, xss, xrs, css, crs, rss, rrs, dss, drs,
    ) = refs[: len(refs) - SWAP_REFS[plan is None]]
    swap_refs = refs[len(refs) - SWAP_REFS[plan is None] :]
    width, tokens = tok_h.shape
    me = lax.axis_index("expert")
    dp = lax.axis_index("dp")
    yy, zl, cc = lax.div(dp, 4), lax.rem(lax.div(dp, 2), 2), lax.rem(dp, 2)

    def at_y(v):
        return v * 4 + zl * 2 + cc

    ya = yy + 1 - 2 * lax.rem(yy, 2)
    yb = 3 - yy
    yc = lax.rem(yy + 2, 4)
    dev_c = {"dp": dp + 1 - 2 * cc}
    dpz = dp + 2 - 4 * zl
    dev_z = {"dp": dpz}
    dev_ya = {"dp": at_y(ya)}
    dev_yb = {"dp": at_y(yb)}

    loads = [
        pltpu.make_async_copy(tok_h, tok, loc.at[0]),
        pltpu.make_async_copy(wg_h.at[0], wg, loc.at[1]),
        pltpu.make_async_copy(wu_h.at[0], wu, loc.at[2]),
        pltpu.make_async_copy(wd_h.at[0], wd, loc.at[3]),
    ]
    for c in loads:
        c.start()

    barrier = pltpu.get_barrier_semaphore()

    def hello(t, _):
        pl.semaphore_signal(barrier, inc=1, device_id={"expert": lax.rem(me + t, N)}, device_id_type=MESH)
        return 0

    def hello_z(t, _):
        dev = {"dp": dpz, "expert": lax.rem(me + t, N)}
        pl.semaphore_signal(barrier, inc=1, device_id=dev, device_id_type=MESH)
        return 0

    lax.fori_loop(1, N, hello, 0)
    other = N if plan is None else 1
    lax.fori_loop(0, other, hello_z, 0)
    for d in (dev_c, dev_ya, dev_yb):
        pl.semaphore_signal(barrier, inc=1, device_id=d, device_id_type=MESH)
    pl.semaphore_wait(barrier, N - 1 + other + 3)

    def turn(t):
        return lax.rem(me + 5 * t, N)

    def cols(i, n=128):
        return pl.ds(pl.multiple_of(i * n, n), n)

    weights, placed = (wg_h, wu_h, wd_h), (pg, pu, pd)
    if plan is None:
        swap = spread_swap(me, dpz, cols, turn, partner, weights, placed, *swap_refs)
    else:
        swap = row_swap(plan, me, partner, weights, placed, *swap_refs)
    swap(0)

    e_of = iota((N, tokens), 0)
    named = jnp.zeros((N, tokens), I32)
    gate = jnp.zeros((N, tokens), F32)
    for j in range(ids.shape[0]):
        eq = ids[j : j + 1, :] == e_of
        named = jnp.where(eq, 1, named)
        gate = jnp.where(eq, gates[j : j + 1, :], gate)
    run = named
    lane = iota((N, tokens), 1)
    step = 1
    while step < tokens:
        run = run + jnp.where(lane >= step, pltpu.roll(run, step, 1), 0)
        step *= 2
    key[...] = jnp.where(named > 0, run - 1, -1)
    gat[...] = gate

    loads[0].wait()
    row_of = iota((MOST, tokens), 0)

    def dispatch(t, _):
        e = turn(t)
        krow = key[pl.ds(e, 1), :]
        pick = (row_of == krow).astype(F32).astype(BF16)
        rows = lax.dot_general(pick, tok[...], LANES, preferred_element_type=F32).astype(BF16)
        total = jnp.sum(jnp.where(krow >= 0, 1.0, 0.0), axis=1, keepdims=True)
        total = jnp.broadcast_to(total, (8, 128))

        @pl.when(t > 0)
        def _():
            xs[e] = rows
            cs[e] = total
            rcopy(cs.at[e], cr.at[me], css.at[t], crs.at[me], {"expert": e}).start()
            rcopy(xs.at[e], xr.at[me], xss.at[t], xrs.at[me], {"expert": e}).start()

        @pl.when(t == 0)
        def _():
            xr[e] = rows
            cr[e] = total

        return 0

    lax.fori_loop(0, N, dispatch, 0)

    swap(1)

    def spread(e, _):
        krow = key[pl.ds(e, 1), :]
        full = jnp.where(row_of == krow, gat[pl.ds(e, 1), :], 0.0)
        hi = full.astype(BF16)
        at = pl.ds(pl.multiple_of(e * MOST, MOST), MOST)
        whi[at, :] = hi
        wlo[at, :] = (full - hi.astype(F32)).astype(BF16)
        return 0

    lax.fori_loop(0, N, spread, 0)

    swap(2)

    def x_wait(t, _):
        b = turn(t)
        rcopy(cs.at[b], cr.at[b], css.at[t], crs.at[b], {"expert": b}).wait_recv()
        rcopy(xs.at[b], xr.at[b], xss.at[t], xrs.at[b], {"expert": b}).wait_recv()
        return 0

    lax.fori_loop(1, N, x_wait, 0)

    limit = capacity[partner[me]].astype(F32)
    p_of = iota((CAP, 2 * MOST), 0).astype(F32)
    l_of = iota((CAP, 2 * MOST), 1)
    i_of = lax.rem(l_of, MOST).astype(F32)

    def place(q, off):
        c0, c1 = cr[2 * q][0:1, 0:1], cr[2 * q + 1][0:1, 0:1]
        offs[2 * q] = jnp.broadcast_to(off, (8, 128))
        offs[2 * q + 1] = jnp.broadcast_to(off + c0, (8, 128))
        count = jnp.where(l_of < MOST, c0, c1)
        start = jnp.where(l_of < MOST, off, off + c0)
        hit = (p_of == start + i_of) & (i_of < count) & (p_of < limit)
        pm[:, cols(q)] = jnp.where(hit, 1.0, 0.0).astype(BF16)
        return off + c0 + c1

    lax.fori_loop(0, N // 2, place, jnp.zeros((1, 1), F32))
    picked[...] = jnp.dot(
        pm[...], xr[...].reshape(N * MOST, width), preferred_element_type=F32
    ).astype(BF16)

    half = wg.shape[1] // 2
    loads[1].wait()
    loads[2].wait()

    def theirs(j, _):
        for w, ref in enumerate((wg, wu)):
            at = pl.ds(pl.multiple_of((1 - cc) * half + j * 256, 256), 256)
            cbs[w, :, cols(j, 256)] = jnp.dot(picked[...], ref[:, at], preferred_element_type=F32)
        return 0

    def ours(j, _):
        for w, ref in enumerate((wg, wu)):
            at = pl.ds(pl.multiple_of(cc * half + j * 256, 256), 256)
            acc[w, :, cols(j, 256)] = jnp.dot(picked[...], ref[:, at], preferred_element_type=F32)
        return 0

    lax.fori_loop(0, half // 256, theirs, 0)
    to_c = rcopy(cbs, cbr, dss.at[0], drs.at[0], dev_c)
    to_c.start()
    swap(3)
    lax.fori_loop(0, half // 256, ours, 0)
    to_c.wait_recv()

    def block(w, q):
        at = cols(q, 256)
        return acc[w, :, at] + cbr[w, :, at]

    y1 = []
    for w, (q, dev) in enumerate(((ya, dev_ya), (yb, dev_yb))):
        y1s[w, 0] = block(w, q).astype(BF16)
        y1s[w, 1] = block(w, yc).astype(BF16)
        c = rcopy(y1s.at[w], y1r.at[w], dss.at[1 + w], drs.at[1 + w], dev)
        c.start()
        y1.append(c)
    swap(4)
    y2 = []
    for w, (q, dev) in enumerate(((yb, dev_yb), (ya, dev_ya))):
        y1[w].wait_recv()
        y2s[w] = (block(w, q) + y1r[w, 1].astype(F32)).astype(BF16)
        c = rcopy(y2s.at[w], y2r.at[w], dss.at[3 + w], drs.at[3 + w], dev)
        c.start()
        y2.append(c)
    swap(5)
    for w in range(2):
        acc[w, :, cols(yy, 256)] = block(w, yy) + y1r[w, 0].astype(F32)
    for w in range(2):
        y2[w].wait_recv()
        y2f = y2r[w].astype(F32)
        lo, hi = y2f[:, :128], y2f[:, 128:]
        away = pl.ds(pl.multiple_of(yy * 256 + (1 - zl) * 128, 128), 128)
        here = pl.ds(pl.multiple_of(yy * 256 + zl * 128, 128), 128)
        zs[w] = (acc[w, :, away] + jnp.where(zl == 0, hi, lo)).astype(BF16)
        acc[w, :, here] = acc[w, :, here] + jnp.where(zl == 0, lo, hi)
    to_z = rcopy(zs, zr, dss.at[5], drs.at[5], dev_z)
    to_z.start()
    to_z.wait_recv()
    here = pl.ds(pl.multiple_of(yy * 256 + zl * 128, 128), 128)
    gsum = acc[0, :, here] + zr[0].astype(F32)
    usum = acc[1, :, here] + zr[1].astype(F32)
    own = cols(cc * 8 + yy * 2 + zl)
    hid[:, own] = (gsum / (1.0 + jnp.exp(-gsum)) * usum).astype(BF16)

    def chunk(c, q):
        return cols(c * 4 + q, 256)

    h_z = rcopy(hid.at[:, own], hid.at[:, own], dss.at[6], drs.at[6], dev_z)
    h_z.start()
    h_z_in = cols(cc * 8 + yy * 2 + 1 - zl)
    rcopy(hid.at[:, h_z_in], hid.at[:, h_z_in], dss.at[6], drs.at[6], dev_z).wait_recv()
    me_q = chunk(cc, yy)

    def to(at, k, dev):
        return rcopy(hid.at[at[0], at[1]], hid.at[at[0], at[1]], dss.at[k], drs.at[k], dev)

    everyrow, top, low = pl.ds(0, CAP), pl.ds(0, CAP // 2), pl.ds(CAP // 2, CAP // 2)
    h_ya = to((everyrow, me_q), 7, dev_ya)
    h_yb = to((everyrow, me_q), 8, dev_yb)
    h_ya.start()
    h_yb.start()
    h_c0 = to((everyrow, me_q), 9, dev_c)
    h_c0.start()
    swap(6)
    to((everyrow, chunk(cc, ya)), 7, dev_ya).wait_recv()
    h_fa = to((top, chunk(cc, ya)), 10, dev_yb)
    h_fa.start()
    h_c1 = to((everyrow, chunk(cc, ya)), 11, dev_c)
    h_c1.start()
    to((everyrow, chunk(cc, yb)), 8, dev_yb).wait_recv()
    h_fb = to((low, chunk(cc, yb)), 12, dev_ya)
    h_fb.start()
    h_c2 = to((everyrow, chunk(cc, yb)), 13, dev_c)
    h_c2.start()
    to((top, chunk(cc, yc)), 10, dev_yb).wait_recv()
    to((low, chunk(cc, yc)), 12, dev_ya).wait_recv()
    h_c3 = to((everyrow, chunk(cc, yc)), 14, dev_c)
    h_c3.start()
    to((everyrow, chunk(1 - cc, yy)), 9, dev_c).wait_recv()
    to((everyrow, chunk(1 - cc, ya)), 11, dev_c).wait_recv()
    to((everyrow, chunk(1 - cc, yb)), 13, dev_c).wait_recv()
    to((everyrow, chunk(1 - cc, yc)), 14, dev_c).wait_recv()

    loads[3].wait()
    swap(7)
    eo[...] = lax.dot_general(hid[...], wd[...], LANES, preferred_element_type=F32).astype(BF16)

    i_row = iota((MOST, CAP), 0).astype(F32)
    p_lane = iota((MOST, CAP), 1).astype(F32)

    def reply(t, _):
        b = turn(t)
        count, start = cr[b][0:1, 0:1], offs[b][0:1, 0:1]
        hit = (p_lane == start + i_row) & (i_row < count) & (p_lane < limit)
        rows = jnp.dot(
            jnp.where(hit, 1.0, 0.0).astype(BF16), eo[...], preferred_element_type=F32
        ).astype(BF16)

        @pl.when(t > 0)
        def _():
            rs[b] = rows
            rcopy(rs.at[b], rr.at[me], rss.at[t], rrs.at[me], {"expert": b}).start()

        @pl.when(t == 0)
        def _():
            rr[b] = rows

        return 0

    lax.fori_loop(0, N, reply, 0)

    swap(8)

    def r_wait(t, _):
        b = turn(t)
        rcopy(rs.at[b], rr.at[b], rss.at[t], rrs.at[b], {"expert": b}).wait_recv()
        return 0

    lax.fori_loop(1, N, r_wait, 0)

    def combine(j, _):
        at = cols(j, 256)
        back = rr[...].reshape(N * MOST, width)
        total = lax.dot_general(back, whi[:, at], ROWS, preferred_element_type=F32)
        total = total + lax.dot_general(back, wlo[:, at], ROWS, preferred_element_type=F32)
        mixed[:, at] = total.astype(BF16)
        return 0

    lax.fori_loop(0, tokens // 256, combine, 0)

    swap(9)

    def sent(t, _):
        i = turn(t)
        rcopy(cs.at[i], cr.at[me], css.at[t], crs.at[me], {"expert": i}).wait_send()
        rcopy(xs.at[i], xr.at[me], xss.at[t], xrs.at[me], {"expert": i}).wait_send()
        rcopy(rs.at[i], rr.at[me], rss.at[t], rrs.at[me], {"expert": i}).wait_send()
        return 0

    lax.fori_loop(1, N, sent, 0)
    for c in (to_c, *y1, *y2, to_z, h_z, h_ya, h_yb, h_c0, h_fa, h_c1, h_fb, h_c2, h_c3):
        c.wait_send()


def layer(plan, rows, width, ff, *args):
    vmem = pl.BlockSpec(memory_space=pltpu.VMEM)
    smem = pl.BlockSpec(memory_space=pltpu.SMEM)
    anyw = pl.BlockSpec(memory_space=pl.ANY)
    V, D = pltpu.VMEM, pltpu.SemaphoreType.DMA
    quarter = ff // 4
    if plan is None:
        swap_scratch = [V((3, N, width, ff // N), BF16)] * 2 + [D((3, N))] * 4
    else:
        near, far = plan
        half = max(far, 1)
        swap_scratch = [
            *[V((4, width, quarter), BF16)] * 3, *[V((2 * near + far, width, quarter), BF16)] * 3,
            V((3, 2 * near + far, width, quarter), BF16),
            V((3, 2, half, width, quarter // 2), BF16), V((3, 4, width, quarter), BF16), V((3, width, quarter), BF16),
            D((6,)), D((3, 32)), D((3, 32)),
        ]
    return pl.pallas_call(
        functools.partial(kernel, plan),
        out_shape=(
            jax.ShapeDtypeStruct((width, rows), BF16),
            jax.ShapeDtypeStruct((1, width, ff), BF16),
            jax.ShapeDtypeStruct((1, width, ff), BF16),
            jax.ShapeDtypeStruct((1, width, ff), BF16),
        ),
        in_specs=[vmem, vmem, smem, smem, anyw, anyw, anyw, anyw],
        out_specs=(vmem, anyw, anyw, anyw),
        scratch_shapes=[
            V((width, rows), BF16), V((width, ff), BF16), V((width, ff), BF16), V((width, ff), BF16),
            V((N, rows), I32), V((N, rows), F32), V((N * MOST, rows), BF16), V((N * MOST, rows), BF16),
            V((N, MOST, width), BF16), V((N, MOST, width), BF16), V((N, 8, 128), F32), V((N, 8, 128), F32),
            V((N, 8, 128), F32), V((CAP, N * MOST), BF16), V((CAP, width), BF16),
            V((2, CAP, ff // 2), F32), V((2, CAP, ff // 2), F32), V((2, CAP, ff // 2), F32),
            V((2, 2, CAP, 256), BF16), V((2, 2, CAP, 256), BF16), V((2, CAP, 256), BF16), V((2, CAP, 256), BF16),
            V((2, CAP, 128), BF16), V((2, CAP, 128), BF16), V((CAP, ff), BF16), V((CAP, width), BF16),
            V((N, MOST, width), BF16), V((N, MOST, width), BF16),
            D((4,)),
            D((N,)), D((N,)), D((N,)), D((N,)), D((N,)), D((N,)), D((16,)), D((16,)),
        ]
        + swap_scratch,
        compiler_params=pltpu.CompilerParams(
            collective_id=PLANS.index(plan), has_side_effects=True, vmem_limit_bytes=67043328
        ),
        name="moe_swap_" + ("any" if plan is None else "%d%d" % plan),
    )(*args)


def local(tokens, expert_ids, gates, gate_weight, up_weight, down_weight, partner, capacity):
    rows, width = tokens.shape
    ff = gate_weight.shape[2]
    slots = jnp.arange(N, dtype=I32)
    ahead = jnp.remainder(partner // 4 - slots // 4, 4).reshape(4, 4)
    near = jnp.max(jnp.sum((ahead == 1).astype(I32), axis=1))
    far = jnp.max(jnp.sum((ahead == 2).astype(I32), axis=1))
    choice = jnp.int32(len(PLANS) - 1)
    for i, plan in reversed(list(enumerate(PLANS[:-1]))):
        choice = jnp.where((near <= plan[0]) & (far <= plan[1]), i, choice)
    args = (
        expert_ids.T, gates.T, capacity, partner, tokens.T,
        gate_weight, up_weight, down_weight.transpose(0, 2, 1),
    )
    mix, new_gate, new_up, new_down = lax.switch(
        choice, [functools.partial(layer, plan, rows, width, ff) for plan in PLANS], *args
    )
    return mix.T, new_gate, new_up, new_down.transpose(0, 2, 1)


def solution(mesh):
    return jax.shard_map(
        local,
        mesh=mesh,
        in_specs=(
            P("expert", "dp"),
            P("expert", None),
            P("expert", None),
            P("expert", "dp", None),
            P("expert", "dp", None),
            P("expert", None, "dp"),
            P(),
            P(),
        ),
        out_specs=(
            P("expert", "dp"),
            P("expert", "dp", None),
            P("expert", "dp", None),
            P("expert", None, "dp"),
        ),
        check_vma=False,
    )
```

```python
import functools

import jax
import jax.numpy as jnp
from jax import lax
from jax.experimental import pallas as pl
from jax.experimental.pallas import tpu as pltpu
from jax.sharding import PartitionSpec as P

MOST = 64
CAP = 640
N = 16
MESH = pl.DeviceIdType.MESH
F32 = jnp.float32
BF16 = jnp.bfloat16
I32 = jnp.int32
LANES = (((1,), (1,)), ((), ()))
ROWS = (((0,), (0,)), ((), ()))
EARLY = 4
SWAP_REFS = {True: 6, False: 13}
PLANS = ((1, 1), (2, 0), None)


def iota(shape, axis):
    return lax.broadcasted_iota(I32, shape, axis)


def rcopy(src, dst, send, recv, dev):
    return pltpu.make_async_remote_copy(
        src_ref=src, dst_ref=dst, send_sem=send, recv_sem=recv, device_id=dev, device_id_type=MESH
    )


def spread_swap(me, dpz, cols, turn, partner, weights, placed, w1b, w2b, w1ss, w1rs, w2ss, w2rs):
    def w1(i, t, src):
        return [
            rcopy(ref.at[0, :, cols(i)], w1b.at[n, src], w1ss.at[n, t], w1rs.at[n, src], {"dp": dpz, "expert": i})
            for n, ref in enumerate(weights)
        ]

    def w2(k, t, src):
        return [
            rcopy(w2b.at[n, k], ref.at[0, :, cols(src)], w2ss.at[n, t], w2rs.at[n, src], {"dp": dpz, "expert": k})
            for n, ref in enumerate(placed)
        ]

    def w1_send(t, _):
        for c in w1(turn(t), t, me):
            c.start()
        return 0

    def w1_wait(t, _):
        for c in w1(me, t, turn(t)):
            c.wait_recv()
        return 0

    def w2_send(t, _):
        k = turn(t)
        s = partner[k]
        for n in range(3):
            w2b[n, k] = w1b[n, s]
        for c in w2(k, t, me):
            c.start()
        return 0

    def w2_wait(t, _):
        for c in w2(me, t, turn(t)):
            c.wait_recv()
        return 0

    def w_sent(t, _):
        for c in w1(turn(t), t, me) + w2(turn(t), t, me):
            c.wait_send()
        return 0

    def swap(point):
        if point == 1:
            lax.fori_loop(0, N, w1_send, 0)
        if point == 6:
            lax.fori_loop(0, N, w1_wait, 0)
            lax.fori_loop(0, EARLY, w2_send, 0)
        if point == 8:
            lax.fori_loop(EARLY, N, w2_send, 0)
        if point == 9:
            lax.fori_loop(0, N, w2_wait, 0)
            lax.fori_loop(0, N, w_sent, 0)

    return swap


def row_swap(
    plan, me, partner, weights, placed, q0, q1, q2, e0, e1, e2, sbuf, relay, x1relay, x2relay, local_sem, ss, rs
):
    near, far = plan
    row_box, far_box = (q0, q1, q2), (e0, e1, e2)
    r, x = lax.div(me, 4), lax.rem(me, 4)
    rp, rm = lax.rem(r + 1, 4), lax.rem(r + 3, 4)
    xp, xm, xo = lax.rem(x + 1, 4), lax.rem(x + 3, 4), lax.rem(x + 2, 4)
    quarter = q0.shape[2]
    left, right = pl.ds(0, quarter // 2), pl.ds(quarter // 2, quarter // 2)
    opposite = 2 * near

    def at(row, col):
        return {"expert": row * 4 + col}

    def part(ref, j):
        return ref.at[0, :, pl.ds(pl.multiple_of(j * quarter, quarter), quarter)]

    def cut(ref, j, w):
        size = quarter // 2
        return ref.at[0, :, pl.ds(pl.multiple_of(j * quarter + w * size, size), size)]

    def row_at(i):
        return lax.div(partner[i], 4)

    def find(target, k):
        seen, found = 0, 0
        for i in range(4):
            hit = row_at(r * 4 + i) == target
            found = jnp.where(hit & (seen == k), i, found)
            seen = seen + jnp.where(hit, 1, 0)
        return found

    def held(col):
        s = partner[r * 4 + col]
        sr, si = lax.div(s, 4), lax.rem(s, 4)
        order = 0
        for i in range(4):
            order = order + jnp.where((si > i) & (row_at(sr * 4 + i) == r), 1, 0)
        d = lax.rem(sr - r + 4, 4)
        place = jnp.where(d == 3, order, jnp.where(d == 1, near + order, opposite + order))
        return d == 0, si, jnp.minimum(place, e0.shape[0] - 1)

    def x1(n, sender=False):
        return [
            rcopy(part(weights[n], to), row_box[n].at[x if sender else src], ss.at[n, d], rs.at[n, d], at(r, to))
            for d, (to, src) in enumerate(((xp, xm), (xm, xp)))
        ]

    def x1_first(n):
        return [
            rcopy(cut(weights[n], xo, w), x1relay.at[n, w], ss.at[n, 2 + w], rs.at[n, 2 + w], at(r, to))
            for w, to in enumerate((xp, xm))
        ]

    def x1_last(n, sender=False):
        return [
            rcopy(
                x1relay.at[n, w], row_box[n].at[src if sender else xo, :, side],
                ss.at[n, 4 + w], rs.at[n, 4 + w], at(r, to),
            )
            for w, (to, src, side) in enumerate(((xp, xm, left), (xm, xp, right)))
        ]

    def x1_local(n):
        return pltpu.make_async_copy(part(weights[n], x), row_box[n].at[x], local_sem.at[n])

    def z1(n, group):
        out = []
        if group:
            for k in range(near):
                out.append((sbuf.at[n, k], far_box[n].at[k], rp))
                out.append((sbuf.at[n, near + k], far_box[n].at[near + k], rm))
        else:
            for k in range(far):
                out.append((sbuf.at[n, 2 * near + k, :, left], relay.at[n, 0, k], rp))
                out.append((sbuf.at[n, 2 * near + k, :, right], relay.at[n, 1, k], rm))
        first = 6 + 2 * far * group
        return [
            rcopy(a, b, ss.at[n, first + i], rs.at[n, first + i], at(row, x)) for i, (a, b, row) in enumerate(out)
        ]

    def z2(n):
        out = []
        for k in range(far):
            for w, (cut, row) in enumerate(((left, rp), (right, rm))):
                i = 16 + 2 * k + w
                out.append(
                    rcopy(relay.at[n, w, k], far_box[n].at[opposite + k, :, cut], ss.at[n, i], rs.at[n, i], at(row, x))
                )
        return out

    def x2(n, sender=False):
        return [
            rcopy(
                sbuf.at[n, 1 + d], part(placed[n], x if sender else src),
                ss.at[n, 22 + d], rs.at[n, 22 + d], at(r, to),
            )
            for d, (to, src) in enumerate(((xp, xm), (xm, xp)))
        ]

    def x2_first(n):
        return [
            rcopy(sbuf.at[n, 3, :, side], x2relay.at[n, w], ss.at[n, 24 + w], rs.at[n, 24 + w], at(r, to))
            for w, (to, side) in enumerate(((xp, left), (xm, right)))
        ]

    def x2_last(n, sender=False):
        return [
            rcopy(
                x2relay.at[n, w], cut(placed[n], src if sender else xo, w),
                ss.at[n, 26 + w], rs.at[n, 26 + w], at(r, to),
            )
            for w, (to, src) in enumerate(((xp, xm), (xm, xp)))
        ]

    def x2_local(n):
        return pltpu.make_async_copy(sbuf.at[n, 0], part(placed[n], x), local_sem.at[3 + n])

    def x1_send(n):
        for c in x1_first(n) + x1(n, True):
            c.start()
        x1_local(n).start()

    def x1_relay(n):
        for c, d in zip(x1_first(n), x1_last(n, True)):
            c.wait_recv()
            d.start()

    def z1_send(n):
        for c in x1(n) + x1_last(n):
            c.wait_recv()
        x1_local(n).wait()
        for k in range(far):
            sbuf[n, 2 * near + k] = row_box[n][find(lax.rem(r + 2, 4), k)]
        for k in range(near):
            sbuf[n, k] = row_box[n][find(rp, k)]
            sbuf[n, near + k] = row_box[n][find(rm, k)]
        for c in z1(n, 0) + z1(n, 1):
            c.start()

    def z2_send(n):
        for c, d in zip(z1(n, 0), z2(n)):
            c.wait_recv()
            d.start()

    def x2_send(n):
        for c in z1(n, 1) + z2(n):
            c.wait_recv()
        for c in z1(n, 0) + z1(n, 1):
            c.wait_send()
        for j, col in enumerate((x, xp, xm, xo)):
            stays, si, place = held(col)
            sbuf[n, j] = jnp.where(stays, row_box[n][si], far_box[n][place])
        for c in x2_first(n) + x2(n, True):
            c.start()
        x2_local(n).start()

    def x2_relay(n):
        for c, d in zip(x2_first(n), x2_last(n, True)):
            c.wait_recv()
            d.start()

    def finish(n):
        for c in x2(n) + x2_last(n):
            c.wait_recv()
        x2_local(n).wait()
        for c in x1_first(n) + x1(n, True) + x1_last(n, True) + z2(n):
            c.wait_send()
        for c in x2_first(n) + x2(n, True) + x2_last(n, True):
            c.wait_send()

    def swap(point):
        if point == 0:
            x1_send(0)
        if point == 10:
            x1_relay(0)
        if point == 1:
            x1_send(1)
        if point == 2:
            z1_send(0)
            x1_relay(1)
            x1_send(2)
            z1_send(1)
        if point == 3:
            x1_relay(2)
        if point == 4:
            z2_send(0)
        if point == 11:
            z2_send(1)
        if point == 6:
            z1_send(2)
            x2_send(0)
        if point == 7:
            x2_send(1)
            z2_send(2)
        if point == 8:
            x2_relay(0)
            x2_relay(1)
            x2_send(2)
            x2_relay(2)
        if point == 9:
            for n in range(3):
                finish(n)

    return swap


def kernel(plan, *refs):
    (
        ids, gates, capacity, partner, tok_h, wg_h, wu_h, wd_h,
        mixed, pg, pu, pd,
        tok, wg, wu, wd, key, gat, whi, wlo,
        xs, xr, cs, cr, offs, pm, picked,
        cbs, cbr, acc, y1s, y1r, y2s, y2r, zs, zr, hid, eo, rs, rr,
        loc, xss, xrs, css, crs, rss, rrs, dss, drs,
    ) = refs[: len(refs) - SWAP_REFS[plan is None]]
    swap_refs = refs[len(refs) - SWAP_REFS[plan is None] :]
    width, tokens = tok_h.shape
    me = lax.axis_index("expert")
    dp = lax.axis_index("dp")
    yy, zl, cc = lax.div(dp, 4), lax.rem(lax.div(dp, 2), 2), lax.rem(dp, 2)

    def at_y(v):
        return v * 4 + zl * 2 + cc

    ya = yy + 1 - 2 * lax.rem(yy, 2)
    yb = 3 - yy
    yc = lax.rem(yy + 2, 4)
    dev_c = {"dp": dp + 1 - 2 * cc}
    dpz = dp + 2 - 4 * zl
    dev_z = {"dp": dpz}
    dev_ya = {"dp": at_y(ya)}
    dev_yb = {"dp": at_y(yb)}

    loads = [
        pltpu.make_async_copy(tok_h, tok, loc.at[0]),
        pltpu.make_async_copy(wg_h.at[0], wg, loc.at[1]),
        pltpu.make_async_copy(wu_h.at[0], wu, loc.at[2]),
        pltpu.make_async_copy(wd_h.at[0], wd, loc.at[3]),
    ]
    for c in loads:
        c.start()

    barrier = pltpu.get_barrier_semaphore()

    def hello(t, _):
        pl.semaphore_signal(barrier, inc=1, device_id={"expert": lax.rem(me + t, N)}, device_id_type=MESH)
        return 0

    def hello_z(t, _):
        dev = {"dp": dpz, "expert": lax.rem(me + t, N)}
        pl.semaphore_signal(barrier, inc=1, device_id=dev, device_id_type=MESH)
        return 0

    lax.fori_loop(1, N, hello, 0)
    other = N if plan is None else 1
    lax.fori_loop(0, other, hello_z, 0)
    for d in (dev_c, dev_ya, dev_yb):
        pl.semaphore_signal(barrier, inc=1, device_id=d, device_id_type=MESH)
    pl.semaphore_wait(barrier, N - 1 + other + 3)

    def turn(t):
        return lax.rem(me + 5 * t, N)

    def cols(i, n=128):
        return pl.ds(pl.multiple_of(i * n, n), n)

    weights, placed = (wg_h, wu_h, wd_h), (pg, pu, pd)
    if plan is None:
        swap = spread_swap(me, dpz, cols, turn, partner, weights, placed, *swap_refs)
    else:
        swap = row_swap(plan, me, partner, weights, placed, *swap_refs)
    swap(0)

    e_of = iota((N, tokens), 0)
    named = jnp.zeros((N, tokens), I32)
    gate = jnp.zeros((N, tokens), F32)
    for j in range(ids.shape[0]):
        eq = ids[j : j + 1, :] == e_of
        named = jnp.where(eq, 1, named)
        gate = jnp.where(eq, gates[j : j + 1, :], gate)
    run = named
    lane = iota((N, tokens), 1)
    step = 1
    while step < tokens:
        run = run + jnp.where(lane >= step, pltpu.roll(run, step, 1), 0)
        step *= 2
    key[...] = jnp.where(named > 0, run - 1, -1)
    gat[...] = gate

    loads[0].wait()
    row_of = iota((MOST, tokens), 0)

    def dispatch(t, _):
        e = turn(t)
        krow = key[pl.ds(e, 1), :]
        pick = (row_of == krow).astype(F32).astype(BF16)
        rows = lax.dot_general(pick, tok[...], LANES, preferred_element_type=F32).astype(BF16)
        total = jnp.sum(jnp.where(krow >= 0, 1.0, 0.0), axis=1, keepdims=True)
        total = jnp.broadcast_to(total, (8, 128))

        @pl.when(t > 0)
        def _():
            xs[e] = rows
            cs[e] = total
            rcopy(cs.at[e], cr.at[me], css.at[t], crs.at[me], {"expert": e}).start()
            rcopy(xs.at[e], xr.at[me], xss.at[t], xrs.at[me], {"expert": e}).start()

        @pl.when(t == 0)
        def _():
            xr[e] = rows
            cr[e] = total

        return 0

    swap(10)
    lax.fori_loop(0, N, dispatch, 0)

    swap(1)

    def spread(e, _):
        krow = key[pl.ds(e, 1), :]
        full = jnp.where(row_of == krow, gat[pl.ds(e, 1), :], 0.0)
        hi = full.astype(BF16)
        at = pl.ds(pl.multiple_of(e * MOST, MOST), MOST)
        whi[at, :] = hi
        wlo[at, :] = (full - hi.astype(F32)).astype(BF16)
        return 0

    lax.fori_loop(0, N, spread, 0)

    swap(2)

    def x_wait(t, _):
        b = turn(t)
        rcopy(cs.at[b], cr.at[b], css.at[t], crs.at[b], {"expert": b}).wait_recv()
        rcopy(xs.at[b], xr.at[b], xss.at[t], xrs.at[b], {"expert": b}).wait_recv()
        return 0

    lax.fori_loop(1, N, x_wait, 0)

    limit = capacity[partner[me]].astype(F32)
    p_of = iota((CAP, 2 * MOST), 0).astype(F32)
    l_of = iota((CAP, 2 * MOST), 1)
    i_of = lax.rem(l_of, MOST).astype(F32)

    def place(q, off):
        c0, c1 = cr[2 * q][0:1, 0:1], cr[2 * q + 1][0:1, 0:1]
        offs[2 * q] = jnp.broadcast_to(off, (8, 128))
        offs[2 * q + 1] = jnp.broadcast_to(off + c0, (8, 128))
        count = jnp.where(l_of < MOST, c0, c1)
        start = jnp.where(l_of < MOST, off, off + c0)
        hit = (p_of == start + i_of) & (i_of < count) & (p_of < limit)
        pm[:, cols(q)] = jnp.where(hit, 1.0, 0.0).astype(BF16)
        return off + c0 + c1

    lax.fori_loop(0, N // 2, place, jnp.zeros((1, 1), F32))
    picked[...] = jnp.dot(
        pm[...], xr[...].reshape(N * MOST, width), preferred_element_type=F32
    ).astype(BF16)

    half = wg.shape[1] // 2
    loads[1].wait()
    loads[2].wait()

    def theirs(j, _):
        for w, ref in enumerate((wg, wu)):
            at = pl.ds(pl.multiple_of((1 - cc) * half + j * 256, 256), 256)
            cbs[w, :, cols(j, 256)] = jnp.dot(picked[...], ref[:, at], preferred_element_type=F32)
        return 0

    def ours(j, _):
        for w, ref in enumerate((wg, wu)):
            at = pl.ds(pl.multiple_of(cc * half + j * 256, 256), 256)
            acc[w, :, cols(j, 256)] = jnp.dot(picked[...], ref[:, at], preferred_element_type=F32)
        return 0

    lax.fori_loop(0, half // 256, theirs, 0)
    to_c = rcopy(cbs, cbr, dss.at[0], drs.at[0], dev_c)
    to_c.start()
    swap(3)
    lax.fori_loop(0, half // 256, ours, 0)
    to_c.wait_recv()

    def block(w, q):
        at = cols(q, 256)
        return acc[w, :, at] + cbr[w, :, at]

    y1 = []
    for w, (q, dev) in enumerate(((ya, dev_ya), (yb, dev_yb))):
        y1s[w, 0] = block(w, q).astype(BF16)
        y1s[w, 1] = block(w, yc).astype(BF16)
        c = rcopy(y1s.at[w], y1r.at[w], dss.at[1 + w], drs.at[1 + w], dev)
        c.start()
        y1.append(c)
    swap(4)
    y2 = []
    for w, (q, dev) in enumerate(((yb, dev_yb), (ya, dev_ya))):
        y1[w].wait_recv()
        y2s[w] = (block(w, q) + y1r[w, 1].astype(F32)).astype(BF16)
        c = rcopy(y2s.at[w], y2r.at[w], dss.at[3 + w], drs.at[3 + w], dev)
        c.start()
        y2.append(c)
    for w in range(2):
        acc[w, :, cols(yy, 256)] = block(w, yy) + y1r[w, 0].astype(F32)
    for w in range(2):
        y2[w].wait_recv()
        y2f = y2r[w].astype(F32)
        lo, hi = y2f[:, :128], y2f[:, 128:]
        away = pl.ds(pl.multiple_of(yy * 256 + (1 - zl) * 128, 128), 128)
        here = pl.ds(pl.multiple_of(yy * 256 + zl * 128, 128), 128)
        zs[w] = (acc[w, :, away] + jnp.where(zl == 0, hi, lo)).astype(BF16)
        acc[w, :, here] = acc[w, :, here] + jnp.where(zl == 0, lo, hi)
    to_z = rcopy(zs, zr, dss.at[5], drs.at[5], dev_z)
    to_z.start()
    swap(11)
    to_z.wait_recv()
    here = pl.ds(pl.multiple_of(yy * 256 + zl * 128, 128), 128)
    gsum = acc[0, :, here] + zr[0].astype(F32)
    usum = acc[1, :, here] + zr[1].astype(F32)
    own = cols(cc * 8 + yy * 2 + zl)
    hid[:, own] = (gsum / (1.0 + jnp.exp(-gsum)) * usum).astype(BF16)

    def chunk(c, q):
        return cols(c * 4 + q, 256)

    h_z = rcopy(hid.at[:, own], hid.at[:, own], dss.at[6], drs.at[6], dev_z)
    h_z.start()
    h_z_in = cols(cc * 8 + yy * 2 + 1 - zl)
    rcopy(hid.at[:, h_z_in], hid.at[:, h_z_in], dss.at[6], drs.at[6], dev_z).wait_recv()
    me_q = chunk(cc, yy)

    def to(at, k, dev):
        return rcopy(hid.at[at[0], at[1]], hid.at[at[0], at[1]], dss.at[k], drs.at[k], dev)

    everyrow, top, low = pl.ds(0, CAP), pl.ds(0, CAP // 2), pl.ds(CAP // 2, CAP // 2)
    h_ya = to((everyrow, me_q), 7, dev_ya)
    h_yb = to((everyrow, me_q), 8, dev_yb)
    h_ya.start()
    h_yb.start()
    h_c0 = to((everyrow, me_q), 9, dev_c)
    h_c0.start()
    swap(6)
    to((everyrow, chunk(cc, ya)), 7, dev_ya).wait_recv()
    h_fa = to((top, chunk(cc, ya)), 10, dev_yb)
    h_fa.start()
    h_c1 = to((everyrow, chunk(cc, ya)), 11, dev_c)
    h_c1.start()
    to((everyrow, chunk(cc, yb)), 8, dev_yb).wait_recv()
    h_fb = to((low, chunk(cc, yb)), 12, dev_ya)
    h_fb.start()
    h_c2 = to((everyrow, chunk(cc, yb)), 13, dev_c)
    h_c2.start()
    to((top, chunk(cc, yc)), 10, dev_yb).wait_recv()
    to((low, chunk(cc, yc)), 12, dev_ya).wait_recv()
    h_c3 = to((everyrow, chunk(cc, yc)), 14, dev_c)
    h_c3.start()
    to((everyrow, chunk(1 - cc, yy)), 9, dev_c).wait_recv()
    to((everyrow, chunk(1 - cc, ya)), 11, dev_c).wait_recv()
    to((everyrow, chunk(1 - cc, yb)), 13, dev_c).wait_recv()
    to((everyrow, chunk(1 - cc, yc)), 14, dev_c).wait_recv()

    loads[3].wait()
    swap(7)
    eo[...] = lax.dot_general(hid[...], wd[...], LANES, preferred_element_type=F32).astype(BF16)

    i_row = iota((MOST, CAP), 0).astype(F32)
    p_lane = iota((MOST, CAP), 1).astype(F32)

    def reply(t, _):
        b = turn(t)
        count, start = cr[b][0:1, 0:1], offs[b][0:1, 0:1]
        hit = (p_lane == start + i_row) & (i_row < count) & (p_lane < limit)
        rows = jnp.dot(
            jnp.where(hit, 1.0, 0.0).astype(BF16), eo[...], preferred_element_type=F32
        ).astype(BF16)

        @pl.when(t > 0)
        def _():
            rs[b] = rows
            rcopy(rs.at[b], rr.at[me], rss.at[t], rrs.at[me], {"expert": b}).start()

        @pl.when(t == 0)
        def _():
            rr[b] = rows

        return 0

    lax.fori_loop(0, N, reply, 0)

    swap(8)

    def r_wait(t, _):
        b = turn(t)
        rcopy(rs.at[b], rr.at[b], rss.at[t], rrs.at[b], {"expert": b}).wait_recv()
        return 0

    lax.fori_loop(1, N, r_wait, 0)

    def combine(j, _):
        at = cols(j, 256)
        back = rr[...].reshape(N * MOST, width)
        total = lax.dot_general(back, whi[:, at], ROWS, preferred_element_type=F32)
        total = total + lax.dot_general(back, wlo[:, at], ROWS, preferred_element_type=F32)
        mixed[:, at] = total.astype(BF16)
        return 0

    lax.fori_loop(0, tokens // 256, combine, 0)

    swap(9)

    def sent(t, _):
        i = turn(t)
        rcopy(cs.at[i], cr.at[me], css.at[t], crs.at[me], {"expert": i}).wait_send()
        rcopy(xs.at[i], xr.at[me], xss.at[t], xrs.at[me], {"expert": i}).wait_send()
        rcopy(rs.at[i], rr.at[me], rss.at[t], rrs.at[me], {"expert": i}).wait_send()
        return 0

    lax.fori_loop(1, N, sent, 0)
    for c in (to_c, *y1, *y2, to_z, h_z, h_ya, h_yb, h_c0, h_fa, h_c1, h_fb, h_c2, h_c3):
        c.wait_send()


def layer(plan, rows, width, ff, *args):
    vmem = pl.BlockSpec(memory_space=pltpu.VMEM)
    smem = pl.BlockSpec(memory_space=pltpu.SMEM)
    anyw = pl.BlockSpec(memory_space=pl.ANY)
    V, D = pltpu.VMEM, pltpu.SemaphoreType.DMA
    quarter = ff // 4
    if plan is None:
        swap_scratch = [V((3, N, width, ff // N), BF16)] * 2 + [D((3, N))] * 4
    else:
        near, far = plan
        half = max(far, 1)
        swap_scratch = [
            *[V((4, width, quarter), BF16)] * 3, *[V((2 * near + far, width, quarter), BF16)] * 3,
            V((3, max(2 * near + far, 4), width, quarter), BF16), V((3, 2, half, width, quarter // 2), BF16),
            V((3, 2, width, quarter // 2), BF16), V((3, 2, width, quarter // 2), BF16),
            D((6,)), D((3, 32)), D((3, 32)),
        ]
    return pl.pallas_call(
        functools.partial(kernel, plan),
        out_shape=(
            jax.ShapeDtypeStruct((width, rows), BF16),
            jax.ShapeDtypeStruct((1, width, ff), BF16),
            jax.ShapeDtypeStruct((1, width, ff), BF16),
            jax.ShapeDtypeStruct((1, width, ff), BF16),
        ),
        in_specs=[vmem, vmem, smem, smem, anyw, anyw, anyw, anyw],
        out_specs=(vmem, anyw, anyw, anyw),
        scratch_shapes=[
            V((width, rows), BF16), V((width, ff), BF16), V((width, ff), BF16), V((width, ff), BF16),
            V((N, rows), I32), V((N, rows), F32), V((N * MOST, rows), BF16), V((N * MOST, rows), BF16),
            V((N, MOST, width), BF16), V((N, MOST, width), BF16), V((N, 8, 128), F32), V((N, 8, 128), F32),
            V((N, 8, 128), F32), V((CAP, N * MOST), BF16), V((CAP, width), BF16),
            V((2, CAP, ff // 2), F32), V((2, CAP, ff // 2), F32), V((2, CAP, ff // 2), F32),
            V((2, 2, CAP, 256), BF16), V((2, 2, CAP, 256), BF16), V((2, CAP, 256), BF16), V((2, CAP, 256), BF16),
            V((2, CAP, 128), BF16), V((2, CAP, 128), BF16), V((CAP, ff), BF16), V((CAP, width), BF16),
            V((N, MOST, width), BF16), V((N, MOST, width), BF16),
            D((4,)),
            D((N,)), D((N,)), D((N,)), D((N,)), D((N,)), D((N,)), D((16,)), D((16,)),
        ]
        + swap_scratch,
        compiler_params=pltpu.CompilerParams(
            collective_id=PLANS.index(plan), has_side_effects=True, vmem_limit_bytes=67043328
        ),
        name="moe_swap_" + ("any" if plan is None else "%d%d" % plan),
    )(*args)


def local(tokens, expert_ids, gates, gate_weight, up_weight, down_weight, partner, capacity):
    rows, width = tokens.shape
    ff = gate_weight.shape[2]
    slots = jnp.arange(N, dtype=I32)
    ahead = jnp.remainder(partner // 4 - slots // 4, 4).reshape(4, 4)
    near = jnp.max(jnp.sum((ahead == 1).astype(I32), axis=1))
    far = jnp.max(jnp.sum((ahead == 2).astype(I32), axis=1))
    choice = jnp.int32(len(PLANS) - 1)
    for i, plan in reversed(list(enumerate(PLANS[:-1]))):
        choice = jnp.where((near <= plan[0]) & (far <= plan[1]), i, choice)
    args = (
        expert_ids.T, gates.T, capacity, partner, tokens.T,
        gate_weight, up_weight, down_weight.transpose(0, 2, 1),
    )
    mix, new_gate, new_up, new_down = lax.switch(
        choice, [functools.partial(layer, plan, rows, width, ff) for plan in PLANS], *args
    )
    return mix.T, new_gate, new_up, new_down.transpose(0, 2, 1)


def solution(mesh):
    return jax.shard_map(
        local,
        mesh=mesh,
        in_specs=(
            P("expert", "dp"),
            P("expert", None),
            P("expert", None),
            P("expert", "dp", None),
            P("expert", "dp", None),
            P("expert", None, "dp"),
            P(),
            P(),
        ),
        out_specs=(
            P("expert", "dp"),
            P("expert", "dp", None),
            P("expert", "dp", None),
            P("expert", None, "dp"),
        ),
        check_vma=False,
    )
```

```python
import functools

import jax
import jax.numpy as jnp
from jax import lax
from jax.experimental import pallas as pl
from jax.experimental.pallas import tpu as pltpu
from jax.sharding import PartitionSpec as P

MOST = 64
CAP = 640
N = 16
MESH = pl.DeviceIdType.MESH
F32 = jnp.float32
BF16 = jnp.bfloat16
I32 = jnp.int32
LANES = (((1,), (1,)), ((), ()))
ROWS = (((0,), (0,)), ((), ()))
EARLY = 4
GROUP = 4
SWAP_REFS = {True: 6, False: 13}
PLANS = ((1, 1), (2, 0), None)


def iota(shape, axis):
    return lax.broadcasted_iota(I32, shape, axis)


def rcopy(src, dst, send, recv, dev):
    return pltpu.make_async_remote_copy(
        src_ref=src, dst_ref=dst, send_sem=send, recv_sem=recv, device_id=dev, device_id_type=MESH
    )


def spread_swap(me, dpz, cols, turn, partner, weights, placed, w1b, w2b, w1ss, w1rs, w2ss, w2rs):
    def w1(i, t, src):
        return [
            rcopy(ref.at[0, :, cols(i)], w1b.at[n, src], w1ss.at[n, t], w1rs.at[n, src], {"dp": dpz, "expert": i})
            for n, ref in enumerate(weights)
        ]

    def w2(k, t, src):
        return [
            rcopy(w2b.at[n, k], ref.at[0, :, cols(src)], w2ss.at[n, t], w2rs.at[n, src], {"dp": dpz, "expert": k})
            for n, ref in enumerate(placed)
        ]

    def w1_send(t, _):
        for c in w1(turn(t), t, me):
            c.start()
        return 0

    def w1_wait(t, _):
        for c in w1(me, t, turn(t)):
            c.wait_recv()
        return 0

    def w2_send(t, _):
        k = turn(t)
        s = partner[k]
        for n in range(3):
            w2b[n, k] = w1b[n, s]
        for c in w2(k, t, me):
            c.start()
        return 0

    def w2_wait(t, _):
        for c in w2(me, t, turn(t)):
            c.wait_recv()
        return 0

    def w_sent(t, _):
        for c in w1(turn(t), t, me) + w2(turn(t), t, me):
            c.wait_send()
        return 0

    def swap(point):
        if point == 1:
            lax.fori_loop(0, N, w1_send, 0)
        if point == 6:
            lax.fori_loop(0, N, w1_wait, 0)
            lax.fori_loop(0, EARLY, w2_send, 0)
        if point == 8:
            lax.fori_loop(EARLY, N, w2_send, 0)
        if point == 9:
            lax.fori_loop(0, N, w2_wait, 0)
            lax.fori_loop(0, N, w_sent, 0)

    return swap


def row_swap(
    plan, me, partner, weights, placed, q0, q1, q2, e0, e1, e2, sbuf, relay, x1relay, x2relay, local_sem, ss, rs
):
    near, far = plan
    row_box, far_box = (q0, q1, q2), (e0, e1, e2)
    r, x = lax.div(me, 4), lax.rem(me, 4)
    rp, rm = lax.rem(r + 1, 4), lax.rem(r + 3, 4)
    xp, xm, xo = lax.rem(x + 1, 4), lax.rem(x + 3, 4), lax.rem(x + 2, 4)
    quarter = q0.shape[2]
    left, right = pl.ds(0, quarter // 2), pl.ds(quarter // 2, quarter // 2)
    opposite = 2 * near

    def at(row, col):
        return {"expert": row * 4 + col}

    def part(ref, j):
        return ref.at[0, :, pl.ds(pl.multiple_of(j * quarter, quarter), quarter)]

    def cut(ref, j, w):
        size = quarter // 2
        return ref.at[0, :, pl.ds(pl.multiple_of(j * quarter + w * size, size), size)]

    def row_at(i):
        return lax.div(partner[i], 4)

    def find(target, k):
        seen, found = 0, 0
        for i in range(4):
            hit = row_at(r * 4 + i) == target
            found = jnp.where(hit & (seen == k), i, found)
            seen = seen + jnp.where(hit, 1, 0)
        return found

    def held(col):
        s = partner[r * 4 + col]
        sr, si = lax.div(s, 4), lax.rem(s, 4)
        order = 0
        for i in range(4):
            order = order + jnp.where((si > i) & (row_at(sr * 4 + i) == r), 1, 0)
        d = lax.rem(sr - r + 4, 4)
        place = jnp.where(d == 3, order, jnp.where(d == 1, near + order, opposite + order))
        return d == 0, si, jnp.minimum(place, e0.shape[0] - 1)

    def x1(n, sender=False):
        return [
            rcopy(part(weights[n], to), row_box[n].at[x if sender else src], ss.at[n, d], rs.at[n, d], at(r, to))
            for d, (to, src) in enumerate(((xp, xm), (xm, xp)))
        ]

    def x1_first(n):
        return [
            rcopy(cut(weights[n], xo, w), x1relay.at[n, w], ss.at[n, 2 + w], rs.at[n, 2 + w], at(r, to))
            for w, to in enumerate((xp, xm))
        ]

    def x1_last(n, sender=False):
        return [
            rcopy(
                x1relay.at[n, w], row_box[n].at[src if sender else xo, :, side],
                ss.at[n, 4 + w], rs.at[n, 4 + w], at(r, to),
            )
            for w, (to, src, side) in enumerate(((xp, xm, left), (xm, xp, right)))
        ]

    def x1_local(n):
        return pltpu.make_async_copy(part(weights[n], x), row_box[n].at[x], local_sem.at[n])

    def z1(n, group):
        out = []
        if group:
            for k in range(near):
                out.append((sbuf.at[n, k], far_box[n].at[k], rp))
                out.append((sbuf.at[n, near + k], far_box[n].at[near + k], rm))
        else:
            for k in range(far):
                out.append((sbuf.at[n, 2 * near + k, :, left], relay.at[n, 0, k], rp))
                out.append((sbuf.at[n, 2 * near + k, :, right], relay.at[n, 1, k], rm))
        first = 6 + 2 * far * group
        return [
            rcopy(a, b, ss.at[n, first + i], rs.at[n, first + i], at(row, x)) for i, (a, b, row) in enumerate(out)
        ]

    def z2(n):
        out = []
        for k in range(far):
            for w, (cut, row) in enumerate(((left, rp), (right, rm))):
                i = 16 + 2 * k + w
                out.append(
                    rcopy(relay.at[n, w, k], far_box[n].at[opposite + k, :, cut], ss.at[n, i], rs.at[n, i], at(row, x))
                )
        return out

    def x2(n, sender=False):
        return [
            rcopy(
                sbuf.at[n, 1 + d], part(placed[n], x if sender else src),
                ss.at[n, 22 + d], rs.at[n, 22 + d], at(r, to),
            )
            for d, (to, src) in enumerate(((xp, xm), (xm, xp)))
        ]

    def x2_first(n):
        return [
            rcopy(sbuf.at[n, 3, :, side], x2relay.at[n, w], ss.at[n, 24 + w], rs.at[n, 24 + w], at(r, to))
            for w, (to, side) in enumerate(((xp, left), (xm, right)))
        ]

    def x2_last(n, sender=False):
        return [
            rcopy(
                x2relay.at[n, w], cut(placed[n], src if sender else xo, w),
                ss.at[n, 26 + w], rs.at[n, 26 + w], at(r, to),
            )
            for w, (to, src) in enumerate(((xp, xm), (xm, xp)))
        ]

    def x2_local(n):
        return pltpu.make_async_copy(sbuf.at[n, 0], part(placed[n], x), local_sem.at[3 + n])

    def x1_send(n):
        for c in x1_first(n) + x1(n, True):
            c.start()
        x1_local(n).start()

    def x1_relay(n):
        for c, d in zip(x1_first(n), x1_last(n, True)):
            c.wait_recv()
            d.start()

    def z1_send(n):
        for c in x1(n) + x1_last(n):
            c.wait_recv()
        x1_local(n).wait()
        for k in range(far):
            sbuf[n, 2 * near + k] = row_box[n][find(lax.rem(r + 2, 4), k)]
        for k in range(near):
            sbuf[n, k] = row_box[n][find(rp, k)]
            sbuf[n, near + k] = row_box[n][find(rm, k)]
        for c in z1(n, 0) + z1(n, 1):
            c.start()

    def z2_send(n):
        for c, d in zip(z1(n, 0), z2(n)):
            c.wait_recv()
            d.start()

    def x2_send(n):
        for c in z1(n, 1) + z2(n):
            c.wait_recv()
        for c in z1(n, 0) + z1(n, 1):
            c.wait_send()
        for j, col in enumerate((x, xp, xm, xo)):
            stays, si, place = held(col)
            sbuf[n, j] = jnp.where(stays, row_box[n][si], far_box[n][place])
        for c in x2_first(n) + x2(n, True):
            c.start()
        x2_local(n).start()

    def x2_relay(n):
        for c, d in zip(x2_first(n), x2_last(n, True)):
            c.wait_recv()
            d.start()

    def finish(n):
        for c in x2(n) + x2_last(n):
            c.wait_recv()
        x2_local(n).wait()
        for c in x1_first(n) + x1(n, True) + x1_last(n, True) + z2(n):
            c.wait_send()
        for c in x2_first(n) + x2(n, True) + x2_last(n, True):
            c.wait_send()

    def swap(point):
        if point == 0:
            x1_send(0)
        if point == 10:
            x1_relay(0)
        if point == 1:
            x1_send(1)
            z1_send(0)
            x1_relay(1)
            x1_send(2)
            z1_send(1)
        if point == 3:
            x1_relay(2)
        if point == 4:
            z2_send(0)
        if point == 11:
            z2_send(1)
        if point == 6:
            z1_send(2)
            x2_send(0)
        if point == 7:
            x2_send(1)
            z2_send(2)
        if point == 8:
            x2_relay(0)
            x2_relay(1)
            x2_send(2)
            x2_relay(2)
        if point == 9:
            for n in range(3):
                finish(n)

    return swap


def kernel(plan, *refs):
    (
        ids, gates, capacity, partner, tok_h, wg_h, wu_h, wd_h,
        mixed, pg, pu, pd,
        tok, wg, wu, wd, key, gat, wsum,
        xs, xr, cs, cr, offs, pm, picked,
        cbs, cbr, acc, y1s, y1r, y2s, y2r, zs, zr, hid, eo, rs, rr,
        loc, xss, xrs, css, crs, rss, rrs, dss, drs,
    ) = refs[: len(refs) - SWAP_REFS[plan is None]]
    swap_refs = refs[len(refs) - SWAP_REFS[plan is None] :]
    width, tokens = tok_h.shape
    me = lax.axis_index("expert")
    dp = lax.axis_index("dp")
    yy, zl, cc = lax.div(dp, 4), lax.rem(lax.div(dp, 2), 2), lax.rem(dp, 2)

    def at_y(v):
        return v * 4 + zl * 2 + cc

    ya = yy + 1 - 2 * lax.rem(yy, 2)
    yb = 3 - yy
    yc = lax.rem(yy + 2, 4)
    dev_c = {"dp": dp + 1 - 2 * cc}
    dpz = dp + 2 - 4 * zl
    dev_z = {"dp": dpz}
    dev_ya = {"dp": at_y(ya)}
    dev_yb = {"dp": at_y(yb)}

    loads = [
        pltpu.make_async_copy(tok_h, tok, loc.at[0]),
        pltpu.make_async_copy(wg_h.at[0], wg, loc.at[1]),
        pltpu.make_async_copy(wu_h.at[0], wu, loc.at[2]),
        pltpu.make_async_copy(wd_h.at[0], wd, loc.at[3]),
    ]
    for c in loads:
        c.start()

    barrier = pltpu.get_barrier_semaphore()

    def hello(t, _):
        pl.semaphore_signal(barrier, inc=1, device_id={"expert": lax.rem(me + t, N)}, device_id_type=MESH)
        return 0

    def hello_z(t, _):
        dev = {"dp": dpz, "expert": lax.rem(me + t, N)}
        pl.semaphore_signal(barrier, inc=1, device_id=dev, device_id_type=MESH)
        return 0

    lax.fori_loop(1, N, hello, 0)
    other = N if plan is None else 1
    lax.fori_loop(0, other, hello_z, 0)
    for d in (dev_c, dev_ya, dev_yb):
        pl.semaphore_signal(barrier, inc=1, device_id=d, device_id_type=MESH)
    pl.semaphore_wait(barrier, N - 1 + other + 3)

    def turn(t):
        return lax.rem(me + 5 * t, N)

    def cols(i, n=128):
        return pl.ds(pl.multiple_of(i * n, n), n)

    weights, placed = (wg_h, wu_h, wd_h), (pg, pu, pd)
    if plan is None:
        swap = spread_swap(me, dpz, cols, turn, partner, weights, placed, *swap_refs)
    else:
        swap = row_swap(plan, me, partner, weights, placed, *swap_refs)
    swap(0)

    e_of = iota((N, tokens), 0)
    named = jnp.zeros((N, tokens), I32)
    gate = jnp.zeros((N, tokens), F32)
    for j in range(ids.shape[0]):
        eq = ids[j : j + 1, :] == e_of
        named = jnp.where(eq, 1, named)
        gate = jnp.where(eq, gates[j : j + 1, :], gate)
    run = named
    lane = iota((N, tokens), 1)
    step = 1
    while step < tokens:
        run = run + jnp.where(lane >= step, pltpu.roll(run, step, 1), 0)
        step *= 2
    key[...] = jnp.where(named > 0, run - 1, -1)
    gat[...] = gate

    loads[0].wait()
    row_of = iota((MOST, tokens), 0)

    def dispatch(g, _):
        slots = [turn(GROUP * g + u) for u in range(GROUP)]
        named_by = [key[pl.ds(e, 1), :] for e in slots]
        pick = jnp.concatenate([(row_of == k).astype(F32).astype(BF16) for k in named_by], axis=0)
        found = lax.dot_general(pick, tok[...], LANES, preferred_element_type=F32).astype(BF16)
        for u, (e, k) in enumerate(zip(slots, named_by)):
            rows = found[u * MOST : (u + 1) * MOST]
            total = jnp.sum(jnp.where(k >= 0, 1.0, 0.0), axis=1, keepdims=True)
            total = jnp.broadcast_to(total, (8, 128))
            t = GROUP * g + u

            def send(e=e, rows=rows, total=total, t=t):
                xs[e] = rows
                cs[e] = total
                rcopy(cs.at[e], cr.at[me], css.at[t], crs.at[me], {"expert": e}).start()
                rcopy(xs.at[e], xr.at[me], xss.at[t], xrs.at[me], {"expert": e}).start()

            def keep(e=e, rows=rows, total=total):
                xr[e] = rows
                cr[e] = total

            if u == 0:
                pl.when(g > 0)(send)
                pl.when(g == 0)(keep)
            else:
                send()
        return 0

    swap(10)
    lax.fori_loop(0, N // GROUP, dispatch, 0)

    swap(1)

    swap(2)

    def x_wait(t, _):
        b = turn(t)
        rcopy(cs.at[b], cr.at[b], css.at[t], crs.at[b], {"expert": b}).wait_recv()
        rcopy(xs.at[b], xr.at[b], xss.at[t], xrs.at[b], {"expert": b}).wait_recv()
        return 0

    lax.fori_loop(1, N, x_wait, 0)

    limit = capacity[partner[me]].astype(F32)
    p_of = iota((CAP, 2 * MOST), 0).astype(F32)
    l_of = iota((CAP, 2 * MOST), 1)
    i_of = lax.rem(l_of, MOST).astype(F32)

    def place(q, off):
        c0, c1 = cr[2 * q][0:1, 0:1], cr[2 * q + 1][0:1, 0:1]
        offs[2 * q] = jnp.broadcast_to(off, (8, 128))
        offs[2 * q + 1] = jnp.broadcast_to(off + c0, (8, 128))
        count = jnp.where(l_of < MOST, c0, c1)
        start = jnp.where(l_of < MOST, off, off + c0)
        hit = (p_of == start + i_of) & (i_of < count) & (p_of < limit)
        pm[:, cols(q)] = jnp.where(hit, 1.0, 0.0).astype(BF16)
        return off + c0 + c1

    lax.fori_loop(0, N // 2, place, jnp.zeros((1, 1), F32))
    picked[...] = jnp.dot(
        pm[...], xr[...].reshape(N * MOST, width), preferred_element_type=F32
    ).astype(BF16)

    half = wg.shape[1] // 2
    loads[1].wait()
    loads[2].wait()

    def theirs(j, _):
        for w, ref in enumerate((wg, wu)):
            at = pl.ds(pl.multiple_of((1 - cc) * half + j * 256, 256), 256)
            cbs[w, :, cols(j, 256)] = jnp.dot(picked[...], ref[:, at], preferred_element_type=F32)
        return 0

    def ours(j, _):
        for w, ref in enumerate((wg, wu)):
            at = pl.ds(pl.multiple_of(cc * half + j * 256, 256), 256)
            acc[w, :, cols(j, 256)] = jnp.dot(picked[...], ref[:, at], preferred_element_type=F32)
        return 0

    lax.fori_loop(0, half // 256, theirs, 0)
    to_c = rcopy(cbs, cbr, dss.at[0], drs.at[0], dev_c)
    to_c.start()
    swap(3)
    lax.fori_loop(0, half // 256, ours, 0)
    to_c.wait_recv()

    def block(w, q):
        at = cols(q, 256)
        return acc[w, :, at] + cbr[w, :, at]

    y1 = []
    for w, (q, dev) in enumerate(((ya, dev_ya), (yb, dev_yb))):
        y1s[w, 0] = block(w, q).astype(BF16)
        y1s[w, 1] = block(w, yc).astype(BF16)
        c = rcopy(y1s.at[w], y1r.at[w], dss.at[1 + w], drs.at[1 + w], dev)
        c.start()
        y1.append(c)
    swap(4)

    def spread(e, _):
        krow = key[pl.ds(e, 1), :]
        full = jnp.where(row_of == krow, gat[pl.ds(e, 1), :], 0.0)
        hi = full.astype(BF16)
        at = pl.ds(pl.multiple_of(e * MOST, MOST), MOST)
        lo = (full - hi.astype(F32)).astype(BF16)
        size = tokens // 2
        for j in range(2):
            wsum[at, 2 * j * size : (2 * j + 1) * size] = hi[:, j * size : (j + 1) * size]
            wsum[at, (2 * j + 1) * size : (2 * j + 2) * size] = lo[:, j * size : (j + 1) * size]
        return 0

    lax.fori_loop(0, N, spread, 0)

    y2 = []
    for w, (q, dev) in enumerate(((yb, dev_yb), (ya, dev_ya))):
        y1[w].wait_recv()
        y2s[w] = (block(w, q) + y1r[w, 1].astype(F32)).astype(BF16)
        c = rcopy(y2s.at[w], y2r.at[w], dss.at[3 + w], drs.at[3 + w], dev)
        c.start()
        y2.append(c)
    for w in range(2):
        acc[w, :, cols(yy, 256)] = block(w, yy) + y1r[w, 0].astype(F32)
    for w in range(2):
        y2[w].wait_recv()
        y2f = y2r[w].astype(F32)
        lo, hi = y2f[:, :128], y2f[:, 128:]
        away = pl.ds(pl.multiple_of(yy * 256 + (1 - zl) * 128, 128), 128)
        here = pl.ds(pl.multiple_of(yy * 256 + zl * 128, 128), 128)
        zs[w] = (acc[w, :, away] + jnp.where(zl == 0, hi, lo)).astype(BF16)
        acc[w, :, here] = acc[w, :, here] + jnp.where(zl == 0, lo, hi)
    to_z = rcopy(zs, zr, dss.at[5], drs.at[5], dev_z)
    to_z.start()
    swap(11)
    to_z.wait_recv()
    here = pl.ds(pl.multiple_of(yy * 256 + zl * 128, 128), 128)
    gsum = acc[0, :, here] + zr[0].astype(F32)
    usum = acc[1, :, here] + zr[1].astype(F32)
    own = cols(cc * 8 + yy * 2 + zl)
    hid[:, own] = (gsum / (1.0 + jnp.exp(-gsum)) * usum).astype(BF16)

    def chunk(c, q):
        return cols(c * 4 + q, 256)

    h_z = rcopy(hid.at[:, own], hid.at[:, own], dss.at[6], drs.at[6], dev_z)
    h_z.start()
    h_z_in = cols(cc * 8 + yy * 2 + 1 - zl)
    rcopy(hid.at[:, h_z_in], hid.at[:, h_z_in], dss.at[6], drs.at[6], dev_z).wait_recv()
    me_q = chunk(cc, yy)

    def to(at, k, dev):
        return rcopy(hid.at[at[0], at[1]], hid.at[at[0], at[1]], dss.at[k], drs.at[k], dev)

    everyrow, top, low = pl.ds(0, CAP), pl.ds(0, CAP // 2), pl.ds(CAP // 2, CAP // 2)
    h_ya = to((everyrow, me_q), 7, dev_ya)
    h_yb = to((everyrow, me_q), 8, dev_yb)
    h_ya.start()
    h_yb.start()
    h_c0 = to((everyrow, me_q), 9, dev_c)
    h_c0.start()
    swap(6)
    to((everyrow, chunk(cc, ya)), 7, dev_ya).wait_recv()
    h_fa = to((top, chunk(cc, ya)), 10, dev_yb)
    h_fa.start()
    h_c1 = to((everyrow, chunk(cc, ya)), 11, dev_c)
    h_c1.start()
    to((everyrow, chunk(cc, yb)), 8, dev_yb).wait_recv()
    h_fb = to((low, chunk(cc, yb)), 12, dev_ya)
    h_fb.start()
    h_c2 = to((everyrow, chunk(cc, yb)), 13, dev_c)
    h_c2.start()
    to((top, chunk(cc, yc)), 10, dev_yb).wait_recv()
    to((low, chunk(cc, yc)), 12, dev_ya).wait_recv()
    h_c3 = to((everyrow, chunk(cc, yc)), 14, dev_c)
    h_c3.start()
    to((everyrow, chunk(1 - cc, yy)), 9, dev_c).wait_recv()
    to((everyrow, chunk(1 - cc, ya)), 11, dev_c).wait_recv()
    to((everyrow, chunk(1 - cc, yb)), 13, dev_c).wait_recv()
    to((everyrow, chunk(1 - cc, yc)), 14, dev_c).wait_recv()

    loads[3].wait()
    swap(7)
    eo[...] = lax.dot_general(hid[...], wd[...], LANES, preferred_element_type=F32).astype(BF16)

    i_row = iota((MOST, CAP), 0).astype(F32)
    p_lane = iota((MOST, CAP), 1).astype(F32)

    def reply(g, _):
        slots = [turn(GROUP * g + u) for u in range(GROUP)]
        places = []
        for b in slots:
            count, start = cr[b][0:1, 0:1], offs[b][0:1, 0:1]
            hit = (p_lane == start + i_row) & (i_row < count) & (p_lane < limit)
            places.append(jnp.where(hit, 1.0, 0.0).astype(BF16))
        found = jnp.dot(
            jnp.concatenate(places, axis=0), eo[...], preferred_element_type=F32
        ).astype(BF16)
        for u, b in enumerate(slots):
            rows = found[u * MOST : (u + 1) * MOST]
            t = GROUP * g + u

            def send(b=b, rows=rows, t=t):
                rs[b] = rows
                rcopy(rs.at[b], rr.at[me], rss.at[t], rrs.at[me], {"expert": b}).start()

            def keep(b=b, rows=rows):
                rr[b] = rows

            if u == 0:
                pl.when(g > 0)(send)
                pl.when(g == 0)(keep)
            else:
                send()
        return 0

    lax.fori_loop(0, N // GROUP, reply, 0)

    swap(8)

    def r_wait(t, _):
        b = turn(t)
        rcopy(rs.at[b], rr.at[b], rss.at[t], rrs.at[b], {"expert": b}).wait_recv()
        return 0

    lax.fori_loop(1, N, r_wait, 0)

    def combine(j, _):
        back = rr[...].reshape(N * MOST, width)
        total = lax.dot_general(back, wsum[:, cols(j, tokens)], ROWS, preferred_element_type=F32)
        mixed[:, cols(j, tokens // 2)] = (total[:, : tokens // 2] + total[:, tokens // 2 :]).astype(BF16)
        return 0

    lax.fori_loop(0, 2, combine, 0)

    swap(9)

    def sent(t, _):
        i = turn(t)
        rcopy(cs.at[i], cr.at[me], css.at[t], crs.at[me], {"expert": i}).wait_send()
        rcopy(xs.at[i], xr.at[me], xss.at[t], xrs.at[me], {"expert": i}).wait_send()
        rcopy(rs.at[i], rr.at[me], rss.at[t], rrs.at[me], {"expert": i}).wait_send()
        return 0

    lax.fori_loop(1, N, sent, 0)
    for c in (to_c, *y1, *y2, to_z, h_z, h_ya, h_yb, h_c0, h_fa, h_c1, h_fb, h_c2, h_c3):
        c.wait_send()


def layer(plan, rows, width, ff, *args):
    vmem = pl.BlockSpec(memory_space=pltpu.VMEM)
    smem = pl.BlockSpec(memory_space=pltpu.SMEM)
    anyw = pl.BlockSpec(memory_space=pl.ANY)
    V, D = pltpu.VMEM, pltpu.SemaphoreType.DMA
    quarter = ff // 4
    if plan is None:
        swap_scratch = [V((3, N, width, ff // N), BF16)] * 2 + [D((3, N))] * 4
    else:
        near, far = plan
        half = max(far, 1)
        swap_scratch = [
            *[V((4, width, quarter), BF16)] * 3, *[V((2 * near + far, width, quarter), BF16)] * 3,
            V((3, max(2 * near + far, 4), width, quarter), BF16), V((3, 2, half, width, quarter // 2), BF16),
            V((3, 2, width, quarter // 2), BF16), V((3, 2, width, quarter // 2), BF16),
            D((6,)), D((3, 32)), D((3, 32)),
        ]
    return pl.pallas_call(
        functools.partial(kernel, plan),
        out_shape=(
            jax.ShapeDtypeStruct((width, rows), BF16),
            jax.ShapeDtypeStruct((1, width, ff), BF16),
            jax.ShapeDtypeStruct((1, width, ff), BF16),
            jax.ShapeDtypeStruct((1, width, ff), BF16),
        ),
        in_specs=[vmem, vmem, smem, smem, anyw, anyw, anyw, anyw],
        out_specs=(vmem, anyw, anyw, anyw),
        scratch_shapes=[
            V((width, rows), BF16), V((width, ff), BF16), V((width, ff), BF16), V((width, ff), BF16),
            V((N, rows), I32), V((N, rows), F32), V((N * MOST, 2 * rows), BF16),
            V((N, MOST, width), BF16), V((N, MOST, width), BF16), V((N, 8, 128), F32), V((N, 8, 128), F32),
            V((N, 8, 128), F32), V((CAP, N * MOST), BF16), V((CAP, width), BF16),
            V((2, CAP, ff // 2), F32), V((2, CAP, ff // 2), F32), V((2, CAP, ff // 2), F32),
            V((2, 2, CAP, 256), BF16), V((2, 2, CAP, 256), BF16), V((2, CAP, 256), BF16), V((2, CAP, 256), BF16),
            V((2, CAP, 128), BF16), V((2, CAP, 128), BF16), V((CAP, ff), BF16), V((CAP, width), BF16),
            V((N, MOST, width), BF16), V((N, MOST, width), BF16),
            D((4,)),
            D((N,)), D((N,)), D((N,)), D((N,)), D((N,)), D((N,)), D((16,)), D((16,)),
        ]
        + swap_scratch,
        compiler_params=pltpu.CompilerParams(
            collective_id=PLANS.index(plan), has_side_effects=True, vmem_limit_bytes=67043328
        ),
        name="moe_swap_" + ("any" if plan is None else "%d%d" % plan),
    )(*args)


def local(tokens, expert_ids, gates, gate_weight, up_weight, down_weight, partner, capacity):
    rows, width = tokens.shape
    ff = gate_weight.shape[2]
    slots = jnp.arange(N, dtype=I32)
    ahead = jnp.remainder(partner // 4 - slots // 4, 4).reshape(4, 4)
    near = jnp.max(jnp.sum((ahead == 1).astype(I32), axis=1))
    far = jnp.max(jnp.sum((ahead == 2).astype(I32), axis=1))
    choice = jnp.int32(len(PLANS) - 1)
    for i, plan in reversed(list(enumerate(PLANS[:-1]))):
        choice = jnp.where((near <= plan[0]) & (far <= plan[1]), i, choice)
    args = (
        expert_ids.T, gates.T, capacity, partner, tokens.T,
        gate_weight, up_weight, down_weight.transpose(0, 2, 1),
    )
    mix, new_gate, new_up, new_down = lax.switch(
        choice, [functools.partial(layer, plan, rows, width, ff) for plan in PLANS], *args
    )
    return mix.T, new_gate, new_up, new_down.transpose(0, 2, 1)


def solution(mesh):
    return jax.shard_map(
        local,
        mesh=mesh,
        in_specs=(
            P("expert", "dp"),
            P("expert", None),
            P("expert", None),
            P("expert", "dp", None),
            P("expert", "dp", None),
            P("expert", None, "dp"),
            P(),
            P(),
        ),
        out_specs=(
            P("expert", "dp"),
            P("expert", "dp", None),
            P("expert", "dp", None),
            P("expert", None, "dp"),
        ),
        check_vma=False,
    )
```

```python
import functools

import jax
import jax.numpy as jnp
from jax import lax
from jax.experimental import pallas as pl
from jax.experimental.pallas import tpu as pltpu
from jax.sharding import PartitionSpec as P

MOST = 64
CAP = 640
N = 16
MESH = pl.DeviceIdType.MESH
F32 = jnp.float32
BF16 = jnp.bfloat16
I32 = jnp.int32
LANES = (((1,), (1,)), ((), ()))
ROWS = (((0,), (0,)), ((), ()))
EARLY = 4
GROUP = 4
SWAP_REFS = {True: 6, False: 13}
PLANS = ((1, 1), (2, 0), None)


def iota(shape, axis):
    return lax.broadcasted_iota(I32, shape, axis)


def rcopy(src, dst, send, recv, dev):
    return pltpu.make_async_remote_copy(
        src_ref=src, dst_ref=dst, send_sem=send, recv_sem=recv, device_id=dev, device_id_type=MESH
    )


def spread_swap(me, dpz, cols, turn, partner, weights, placed, w1b, w2b, w1ss, w1rs, w2ss, w2rs):
    def w1(i, t, src):
        return [
            rcopy(ref.at[0, :, cols(i)], w1b.at[n, src], w1ss.at[n, t], w1rs.at[n, src], {"dp": dpz, "expert": i})
            for n, ref in enumerate(weights)
        ]

    def w2(k, t, src):
        return [
            rcopy(w2b.at[n, k], ref.at[0, :, cols(src)], w2ss.at[n, t], w2rs.at[n, src], {"dp": dpz, "expert": k})
            for n, ref in enumerate(placed)
        ]

    def w1_send(t, _):
        for c in w1(turn(t), t, me):
            c.start()
        return 0

    def w1_wait(t, _):
        for c in w1(me, t, turn(t)):
            c.wait_recv()
        return 0

    def w2_send(t, _):
        k = turn(t)
        s = partner[k]
        for n in range(3):
            w2b[n, k] = w1b[n, s]
        for c in w2(k, t, me):
            c.start()
        return 0

    def w2_wait(t, _):
        for c in w2(me, t, turn(t)):
            c.wait_recv()
        return 0

    def w_sent(t, _):
        for c in w1(turn(t), t, me) + w2(turn(t), t, me):
            c.wait_send()
        return 0

    def swap(point):
        if point == 1:
            lax.fori_loop(0, N, w1_send, 0)
        if point == 6:
            lax.fori_loop(0, N, w1_wait, 0)
            lax.fori_loop(0, EARLY, w2_send, 0)
        if point == 8:
            lax.fori_loop(EARLY, N, w2_send, 0)
        if point == 9:
            lax.fori_loop(0, N, w2_wait, 0)
            lax.fori_loop(0, N, w_sent, 0)

    return swap


def row_swap(
    plan, me, partner, weights, placed, q0, q1, q2, e0, e1, e2, sbuf, relay, x1relay, x2relay, local_sem, ss, rs
):
    near, far = plan
    row_box, far_box = (q0, q1, q2), (e0, e1, e2)
    r, x = lax.div(me, 4), lax.rem(me, 4)
    rp, rm = lax.rem(r + 1, 4), lax.rem(r + 3, 4)
    xp, xm, xo = lax.rem(x + 1, 4), lax.rem(x + 3, 4), lax.rem(x + 2, 4)
    quarter = q0.shape[2]
    left, right = pl.ds(0, quarter // 2), pl.ds(quarter // 2, quarter // 2)
    opposite = 2 * near

    def at(row, col):
        return {"expert": row * 4 + col}

    def part(ref, j):
        return ref.at[0, :, pl.ds(pl.multiple_of(j * quarter, quarter), quarter)]

    def cut(ref, j, w):
        size = quarter // 2
        return ref.at[0, :, pl.ds(pl.multiple_of(j * quarter + w * size, size), size)]

    def row_at(i):
        return lax.div(partner[i], 4)

    def find(target, k):
        seen, found = 0, 0
        for i in range(4):
            hit = row_at(r * 4 + i) == target
            found = jnp.where(hit & (seen == k), i, found)
            seen = seen + jnp.where(hit, 1, 0)
        return found

    def held(col):
        s = partner[r * 4 + col]
        sr, si = lax.div(s, 4), lax.rem(s, 4)
        order = 0
        for i in range(4):
            order = order + jnp.where((si > i) & (row_at(sr * 4 + i) == r), 1, 0)
        d = lax.rem(sr - r + 4, 4)
        place = jnp.where(d == 3, order, jnp.where(d == 1, near + order, opposite + order))
        return d == 0, si, jnp.minimum(place, e0.shape[0] - 1)

    def x1(n, sender=False):
        return [
            rcopy(part(weights[n], to), row_box[n].at[x if sender else src], ss.at[n, d], rs.at[n, d], at(r, to))
            for d, (to, src) in enumerate(((xp, xm), (xm, xp)))
        ]

    def x1_first(n):
        return [
            rcopy(cut(weights[n], xo, w), x1relay.at[n, w], ss.at[n, 2 + w], rs.at[n, 2 + w], at(r, to))
            for w, to in enumerate((xp, xm))
        ]

    def x1_last(n, sender=False):
        return [
            rcopy(
                x1relay.at[n, w], row_box[n].at[src if sender else xo, :, side],
                ss.at[n, 4 + w], rs.at[n, 4 + w], at(r, to),
            )
            for w, (to, src, side) in enumerate(((xp, xm, left), (xm, xp, right)))
        ]

    def x1_local(n):
        return pltpu.make_async_copy(part(weights[n], x), row_box[n].at[x], local_sem.at[n])

    def z1(n, group):
        out = []
        if group:
            for k in range(near):
                out.append((sbuf.at[n, k], far_box[n].at[k], rp))
                out.append((sbuf.at[n, near + k], far_box[n].at[near + k], rm))
        else:
            for k in range(far):
                out.append((sbuf.at[n, 2 * near + k, :, left], relay.at[n, 0, k], rp))
                out.append((sbuf.at[n, 2 * near + k, :, right], relay.at[n, 1, k], rm))
        first = 6 + 2 * far * group
        return [
            rcopy(a, b, ss.at[n, first + i], rs.at[n, first + i], at(row, x)) for i, (a, b, row) in enumerate(out)
        ]

    def z2(n):
        out = []
        for k in range(far):
            for w, (cut, row) in enumerate(((left, rp), (right, rm))):
                i = 16 + 2 * k + w
                out.append(
                    rcopy(relay.at[n, w, k], far_box[n].at[opposite + k, :, cut], ss.at[n, i], rs.at[n, i], at(row, x))
                )
        return out

    def x2(n, sender=False):
        return [
            rcopy(
                sbuf.at[n, 1 + d], part(placed[n], x if sender else src),
                ss.at[n, 22 + d], rs.at[n, 22 + d], at(r, to),
            )
            for d, (to, src) in enumerate(((xp, xm), (xm, xp)))
        ]

    def x2_first(n):
        return [
            rcopy(sbuf.at[n, 3, :, side], x2relay.at[n, w], ss.at[n, 24 + w], rs.at[n, 24 + w], at(r, to))
            for w, (to, side) in enumerate(((xp, left), (xm, right)))
        ]

    def x2_last(n, sender=False):
        return [
            rcopy(
                x2relay.at[n, w], cut(placed[n], src if sender else xo, w),
                ss.at[n, 26 + w], rs.at[n, 26 + w], at(r, to),
            )
            for w, (to, src) in enumerate(((xp, xm), (xm, xp)))
        ]

    def x2_local(n):
        return pltpu.make_async_copy(sbuf.at[n, 0], part(placed[n], x), local_sem.at[3 + n])

    def x1_send(n):
        for c in x1_first(n) + x1(n, True):
            c.start()
        x1_local(n).start()

    def x1_relay(n):
        for c, d in zip(x1_first(n), x1_last(n, True)):
            c.wait_recv()
            d.start()

    def z1_send(n):
        for c in x1(n) + x1_last(n):
            c.wait_recv()
        x1_local(n).wait()
        for k in range(far):
            sbuf[n, 2 * near + k] = row_box[n][find(lax.rem(r + 2, 4), k)]
        for k in range(near):
            sbuf[n, k] = row_box[n][find(rp, k)]
            sbuf[n, near + k] = row_box[n][find(rm, k)]
        for c in z1(n, 0) + z1(n, 1):
            c.start()

    def z2_send(n):
        for c, d in zip(z1(n, 0), z2(n)):
            c.wait_recv()
            d.start()

    def x2_send(n):
        for c in z1(n, 1) + z2(n):
            c.wait_recv()
        for c in z1(n, 0) + z1(n, 1):
            c.wait_send()
        for j, col in enumerate((x, xp, xm, xo)):
            stays, si, place = held(col)
            sbuf[n, j] = jnp.where(stays, row_box[n][si], far_box[n][place])
        for c in x2_first(n) + x2(n, True):
            c.start()
        x2_local(n).start()

    def x2_relay(n):
        for c, d in zip(x2_first(n), x2_last(n, True)):
            c.wait_recv()
            d.start()

    def finish(n):
        for c in x2(n) + x2_last(n):
            c.wait_recv()
        x2_local(n).wait()
        for c in x1_first(n) + x1(n, True) + x1_last(n, True) + z2(n):
            c.wait_send()
        for c in x2_first(n) + x2(n, True) + x2_last(n, True):
            c.wait_send()

    def swap(point):
        if point == 0:
            x1_send(0)
        if point == 10:
            x1_relay(0)
        if point == 1:
            x1_send(1)
            z1_send(0)
            x1_relay(1)
            x1_send(2)
            z1_send(1)
        if point == 3:
            x1_relay(2)
        if point == 4:
            z2_send(0)
        if point == 11:
            z2_send(1)
        if point == 6:
            z1_send(2)
            x2_send(0)
        if point == 7:
            x2_send(1)
            z2_send(2)
        if point == 8:
            x2_relay(0)
            x2_relay(1)
            x2_send(2)
            x2_relay(2)
        if point == 9:
            for n in range(3):
                finish(n)

    return swap


def kernel(plan, *refs):
    (
        ids, gates, capacity, partner, tok_h, wg_h, wu_h, wd_h,
        mixed, pg, pu, pd,
        tok, wg, wu, wd, key, gat, wsum,
        xs, xr, cs, cr, offs, pm, picked,
        cbs, cbr, acc, y1s, y1r, y2s, y2r, zs, zr, hid, eo, rs, rr,
        loc, xss, xrs, css, crs, rss, rrs, dss, drs,
    ) = refs[: len(refs) - SWAP_REFS[plan is None]]
    swap_refs = refs[len(refs) - SWAP_REFS[plan is None] :]
    width, tokens = tok_h.shape
    me = lax.axis_index("expert")
    dp = lax.axis_index("dp")
    yy, zl, cc = lax.div(dp, 4), lax.rem(lax.div(dp, 2), 2), lax.rem(dp, 2)

    def at_y(v):
        return v * 4 + zl * 2 + cc

    ya = yy + 1 - 2 * lax.rem(yy, 2)
    yb = 3 - yy
    yc = lax.rem(yy + 2, 4)
    dev_c = {"dp": dp + 1 - 2 * cc}
    dpz = dp + 2 - 4 * zl
    dev_z = {"dp": dpz}
    dev_ya = {"dp": at_y(ya)}
    dev_yb = {"dp": at_y(yb)}

    loads = [
        pltpu.make_async_copy(tok_h, tok, loc.at[0]),
        pltpu.make_async_copy(wg_h.at[0], wg, loc.at[1]),
        pltpu.make_async_copy(wu_h.at[0], wu, loc.at[2]),
        pltpu.make_async_copy(wd_h.at[0], wd, loc.at[3]),
    ]
    for c in loads:
        c.start()

    barrier = pltpu.get_barrier_semaphore()

    def hello(t, _):
        pl.semaphore_signal(barrier, inc=1, device_id={"expert": lax.rem(me + t, N)}, device_id_type=MESH)
        return 0

    def hello_z(t, _):
        dev = {"dp": dpz, "expert": lax.rem(me + t, N)}
        pl.semaphore_signal(barrier, inc=1, device_id=dev, device_id_type=MESH)
        return 0

    lax.fori_loop(1, N, hello, 0)
    other = N if plan is None else 1
    lax.fori_loop(0, other, hello_z, 0)
    for d in (dev_c, dev_ya, dev_yb):
        pl.semaphore_signal(barrier, inc=1, device_id=d, device_id_type=MESH)
    pl.semaphore_wait(barrier, N - 1 + other + 3)

    def turn(t):
        return lax.rem(me + 5 * t, N)

    def cols(i, n=128):
        return pl.ds(pl.multiple_of(i * n, n), n)

    weights, placed = (wg_h, wu_h, wd_h), (pg, pu, pd)
    if plan is None:
        swap = spread_swap(me, dpz, cols, turn, partner, weights, placed, *swap_refs)
    else:
        swap = row_swap(plan, me, partner, weights, placed, *swap_refs)
    swap(0)

    e_of = iota((N, tokens), 0)
    named = jnp.zeros((N, tokens), I32)
    gate = jnp.zeros((N, tokens), F32)
    for j in range(ids.shape[0]):
        eq = ids[j : j + 1, :] == e_of
        named = jnp.where(eq, 1, named)
        gate = jnp.where(eq, gates[j : j + 1, :], gate)
    run = named
    lane = iota((N, tokens), 1)
    step = 1
    while step < tokens:
        run = run + jnp.where(lane >= step, pltpu.roll(run, step, 1), 0)
        step *= 2
    key[...] = jnp.where(named > 0, run - 1, -1)
    gat[...] = gate

    loads[0].wait()
    row_of = iota((MOST, tokens), 0)

    def dispatch(g, _):
        slots = [turn(GROUP * g + u) for u in range(GROUP)]
        named_by = [key[pl.ds(e, 1), :] for e in slots]
        pick = jnp.concatenate([(row_of == k).astype(F32).astype(BF16) for k in named_by], axis=0)
        found = lax.dot_general(pick, tok[...], LANES, preferred_element_type=F32).astype(BF16)
        for u, (e, k) in enumerate(zip(slots, named_by)):
            rows = found[u * MOST : (u + 1) * MOST]
            total = jnp.sum(jnp.where(k >= 0, 1.0, 0.0), axis=1, keepdims=True)
            total = jnp.broadcast_to(total, (8, 128))
            t = GROUP * g + u

            def send(e=e, rows=rows, total=total, t=t):
                xs[e] = rows
                cs[e] = total
                rcopy(cs.at[e], cr.at[me], css.at[t], crs.at[me], {"expert": e}).start()
                rcopy(xs.at[e], xr.at[me], xss.at[t], xrs.at[me], {"expert": e}).start()

            def keep(e=e, rows=rows, total=total):
                xr[e] = rows
                cr[e] = total

            if u == 0:
                pl.when(g > 0)(send)
                pl.when(g == 0)(keep)
            else:
                send()
        return 0

    swap(10)
    lax.fori_loop(0, N // GROUP, dispatch, 0)

    swap(1)

    swap(2)

    def x_wait(t, _):
        b = turn(t)
        rcopy(cs.at[b], cr.at[b], css.at[t], crs.at[b], {"expert": b}).wait_recv()
        rcopy(xs.at[b], xr.at[b], xss.at[t], xrs.at[b], {"expert": b}).wait_recv()
        return 0

    lax.fori_loop(1, N, x_wait, 0)

    limit = capacity[partner[me]].astype(F32)
    p_of = iota((CAP, 2 * MOST), 0).astype(F32)
    l_of = iota((CAP, 2 * MOST), 1)
    i_of = lax.rem(l_of, MOST).astype(F32)

    def place(q, off):
        c0, c1 = cr[2 * q][0:1, 0:1], cr[2 * q + 1][0:1, 0:1]
        offs[2 * q] = jnp.broadcast_to(off, (8, 128))
        offs[2 * q + 1] = jnp.broadcast_to(off + c0, (8, 128))
        count = jnp.where(l_of < MOST, c0, c1)
        start = jnp.where(l_of < MOST, off, off + c0)
        hit = (p_of == start + i_of) & (i_of < count) & (p_of < limit)
        pm[:, cols(q)] = jnp.where(hit, 1.0, 0.0).astype(BF16)
        return off + c0 + c1

    lax.fori_loop(0, N // 2, place, jnp.zeros((1, 1), F32))
    picked[...] = jnp.dot(
        pm[...], xr[...].reshape(N * MOST, width), preferred_element_type=F32
    ).astype(BF16)

    half = wg.shape[1] // 2
    loads[1].wait()
    loads[2].wait()

    def theirs(j, _):
        for w, ref in enumerate((wg, wu)):
            at = pl.ds(pl.multiple_of((1 - cc) * half + j * 256, 256), 256)
            cbs[w, :, cols(j, 256)] = jnp.dot(picked[...], ref[:, at], preferred_element_type=F32)
        return 0

    def ours(j, _):
        for w, ref in enumerate((wg, wu)):
            at = pl.ds(pl.multiple_of(cc * half + j * 256, 256), 256)
            acc[w, :, cols(j, 256)] = jnp.dot(picked[...], ref[:, at], preferred_element_type=F32)
        return 0

    lax.fori_loop(0, half // 256, theirs, 0)
    to_c = rcopy(cbs, cbr, dss.at[0], drs.at[0], dev_c)
    to_c.start()
    swap(3)
    lax.fori_loop(0, half // 256, ours, 0)
    to_c.wait_recv()

    def block(w, q):
        at = cols(q, 256)
        return acc[w, :, at] + cbr[w, :, at]

    y1 = []
    for w, (q, dev) in enumerate(((ya, dev_ya), (yb, dev_yb))):
        y1s[w, 0] = block(w, q).astype(BF16)
        y1s[w, 1] = block(w, yc).astype(BF16)
        c = rcopy(y1s.at[w], y1r.at[w], dss.at[1 + w], drs.at[1 + w], dev)
        c.start()
        y1.append(c)
    swap(4)

    def spread(e, _):
        krow = key[pl.ds(e, 1), :]
        full = jnp.where(row_of == krow, gat[pl.ds(e, 1), :], 0.0)
        hi = full.astype(BF16)
        at = pl.ds(pl.multiple_of(e * MOST, MOST), MOST)
        lo = (full - hi.astype(F32)).astype(BF16)
        size = tokens // 2
        for j in range(2):
            wsum[at, 2 * j * size : (2 * j + 1) * size] = hi[:, j * size : (j + 1) * size]
            wsum[at, (2 * j + 1) * size : (2 * j + 2) * size] = lo[:, j * size : (j + 1) * size]
        return 0

    lax.fori_loop(0, N, spread, 0)

    y2 = []
    for w, (q, dev) in enumerate(((yb, dev_yb), (ya, dev_ya))):
        y1[w].wait_recv()
        y2s[w] = (block(w, q) + y1r[w, 1].astype(F32)).astype(BF16)
        c = rcopy(y2s.at[w], y2r.at[w], dss.at[3 + w], drs.at[3 + w], dev)
        c.start()
        y2.append(c)
    for w in range(2):
        acc[w, :, cols(yy, 256)] = block(w, yy) + y1r[w, 0].astype(F32)
    for w in range(2):
        y2[w].wait_recv()
        y2f = y2r[w].astype(F32)
        lo, hi = y2f[:, :128], y2f[:, 128:]
        away = pl.ds(pl.multiple_of(yy * 256 + (1 - zl) * 128, 128), 128)
        here = pl.ds(pl.multiple_of(yy * 256 + zl * 128, 128), 128)
        zs[w] = (acc[w, :, away] + jnp.where(zl == 0, hi, lo)).astype(BF16)
        acc[w, :, here] = acc[w, :, here] + jnp.where(zl == 0, lo, hi)
    to_z = rcopy(zs, zr, dss.at[5], drs.at[5], dev_z)
    to_z.start()
    swap(11)
    to_z.wait_recv()
    here = pl.ds(pl.multiple_of(yy * 256 + zl * 128, 128), 128)
    gsum = acc[0, :, here] + zr[0].astype(F32)
    usum = acc[1, :, here] + zr[1].astype(F32)
    own = cols(cc * 8 + yy * 2 + zl)
    hid[:, own] = (gsum / (1.0 + jnp.exp(-gsum)) * usum).astype(BF16)

    def chunk(c, q):
        return cols(c * 4 + q, 256)

    h_z = rcopy(hid.at[:, own], hid.at[:, own], dss.at[6], drs.at[6], dev_z)
    h_z.start()
    h_z_in = cols(cc * 8 + yy * 2 + 1 - zl)
    rcopy(hid.at[:, h_z_in], hid.at[:, h_z_in], dss.at[6], drs.at[6], dev_z).wait_recv()
    me_q = chunk(cc, yy)

    def to(at, k, dev):
        return rcopy(hid.at[at[0], at[1]], hid.at[at[0], at[1]], dss.at[k], drs.at[k], dev)

    everyrow, top, low = pl.ds(0, CAP), pl.ds(0, CAP // 2), pl.ds(CAP // 2, CAP // 2)
    h_ya = to((everyrow, me_q), 7, dev_ya)
    h_yb = to((everyrow, me_q), 8, dev_yb)
    h_ya.start()
    h_yb.start()
    h_c0 = to((everyrow, me_q), 9, dev_c)
    h_c0.start()
    swap(6)
    to((everyrow, chunk(cc, ya)), 7, dev_ya).wait_recv()
    h_fa = to((top, chunk(cc, ya)), 10, dev_yb)
    h_fa.start()
    h_c1 = to((everyrow, chunk(cc, ya)), 11, dev_c)
    h_c1.start()
    to((everyrow, chunk(cc, yb)), 8, dev_yb).wait_recv()
    h_fb = to((low, chunk(cc, yb)), 12, dev_ya)
    h_fb.start()
    h_c2 = to((everyrow, chunk(cc, yb)), 13, dev_c)
    h_c2.start()
    to((top, chunk(cc, yc)), 10, dev_yb).wait_recv()
    to((low, chunk(cc, yc)), 12, dev_ya).wait_recv()
    h_c3 = to((everyrow, chunk(cc, yc)), 14, dev_c)
    h_c3.start()
    to((everyrow, chunk(1 - cc, yy)), 9, dev_c).wait_recv()
    to((everyrow, chunk(1 - cc, ya)), 11, dev_c).wait_recv()
    to((everyrow, chunk(1 - cc, yb)), 13, dev_c).wait_recv()
    to((everyrow, chunk(1 - cc, yc)), 14, dev_c).wait_recv()

    loads[3].wait()
    swap(7)
    eo[...] = lax.dot_general(hid[...], wd[...], LANES, preferred_element_type=F32).astype(BF16)

    i_row = iota((MOST, CAP), 0).astype(F32)
    p_lane = iota((MOST, CAP), 1).astype(F32)

    def reply(g, _):
        slots = [turn(GROUP * g + u) for u in range(GROUP)]
        places = []
        for b in slots:
            count, start = cr[b][0:1, 0:1], offs[b][0:1, 0:1]
            hit = (p_lane == start + i_row) & (i_row < count) & (p_lane < limit)
            places.append(jnp.where(hit, 1.0, 0.0).astype(BF16))
        found = jnp.dot(
            jnp.concatenate(places, axis=0), eo[...], preferred_element_type=F32
        ).astype(BF16)
        for u, b in enumerate(slots):
            rows = found[u * MOST : (u + 1) * MOST]
            t = GROUP * g + u

            def send(b=b, rows=rows, t=t):
                rs[b] = rows
                rcopy(rs.at[b], rr.at[me], rss.at[t], rrs.at[me], {"expert": b}).start()

            def keep(b=b, rows=rows):
                rr[b] = rows

            if u == 0:
                pl.when(g > 0)(send)
                pl.when(g == 0)(keep)
            else:
                send()
        return 0

    lax.fori_loop(0, N // GROUP, reply, 0)

    swap(8)

    def r_wait(t, _):
        b = turn(t)
        rcopy(rs.at[b], rr.at[b], rss.at[t], rrs.at[b], {"expert": b}).wait_recv()
        return 0

    lax.fori_loop(1, N, r_wait, 0)

    def combine(j, _):
        back = rr[...].reshape(N * MOST, width)
        total = lax.dot_general(back, wsum[:, cols(j, tokens)], ROWS, preferred_element_type=F32)
        mixed[:, cols(j, tokens // 2)] = (total[:, : tokens // 2] + total[:, tokens // 2 :]).astype(BF16)
        return 0

    lax.fori_loop(0, 2, combine, 0)

    swap(9)

    def sent(t, _):
        i = turn(t)
        rcopy(cs.at[i], cr.at[me], css.at[t], crs.at[me], {"expert": i}).wait_send()
        rcopy(xs.at[i], xr.at[me], xss.at[t], xrs.at[me], {"expert": i}).wait_send()
        rcopy(rs.at[i], rr.at[me], rss.at[t], rrs.at[me], {"expert": i}).wait_send()
        return 0

    lax.fori_loop(1, N, sent, 0)
    for c in (to_c, *y1, *y2, to_z, h_z, h_ya, h_yb, h_c0, h_fa, h_c1, h_fb, h_c2, h_c3):
        c.wait_send()


def layer(plan, rows, width, ff, *args):
    vmem = pl.BlockSpec(memory_space=pltpu.VMEM)
    smem = pl.BlockSpec(memory_space=pltpu.SMEM)
    anyw = pl.BlockSpec(memory_space=pl.ANY)
    V, D = pltpu.VMEM, pltpu.SemaphoreType.DMA
    quarter = ff // 4
    if plan is None:
        swap_scratch = [V((3, N, width, ff // N), BF16)] * 2 + [D((3, N))] * 4
    else:
        near, far = plan
        half = max(far, 1)
        swap_scratch = [
            *[V((4, width, quarter), BF16)] * 3, *[V((2 * near + far, width, quarter), BF16)] * 3,
            V((3, max(2 * near + far, 4), width, quarter), BF16), V((3, 2, half, width, quarter // 2), BF16),
            V((3, 2, width, quarter // 2), BF16), V((3, 2, width, quarter // 2), BF16),
            D((6,)), D((3, 32)), D((3, 32)),
        ]
    return pl.pallas_call(
        functools.partial(kernel, plan),
        out_shape=(
            jax.ShapeDtypeStruct((width, rows), BF16),
            jax.ShapeDtypeStruct((1, width, ff), BF16),
            jax.ShapeDtypeStruct((1, width, ff), BF16),
            jax.ShapeDtypeStruct((1, width, ff), BF16),
        ),
        in_specs=[vmem, vmem, smem, smem, anyw, anyw, anyw, anyw],
        out_specs=(vmem, anyw, anyw, anyw),
        scratch_shapes=[
            V((width, rows), BF16), V((width, ff), BF16), V((width, ff), BF16), V((width, ff), BF16),
            V((N, rows), I32), V((N, rows), F32), V((N * MOST, 2 * rows), BF16),
            V((N, MOST, width), BF16), V((N, MOST, width), BF16), V((N, 8, 128), F32), V((N, 8, 128), F32),
            V((N, 8, 128), F32), V((CAP, N * MOST), BF16), V((CAP, width), BF16),
            V((2, CAP, ff // 2), F32), V((2, CAP, ff // 2), F32), V((2, CAP, ff // 2), F32),
            V((2, 2, CAP, 256), BF16), V((2, 2, CAP, 256), BF16), V((2, CAP, 256), BF16), V((2, CAP, 256), BF16),
            V((2, CAP, 128), BF16), V((2, CAP, 128), BF16), V((CAP, ff), BF16), V((CAP, width), BF16),
            V((N, MOST, width), BF16), V((N, MOST, width), BF16),
            D((4,)),
            D((N,)), D((N,)), D((N,)), D((N,)), D((N,)), D((N,)), D((16,)), D((16,)),
        ]
        + swap_scratch,
        compiler_params=pltpu.CompilerParams(
            collective_id=PLANS.index(plan), has_side_effects=True, vmem_limit_bytes=67043328
        ),
        name="moe_swap_" + ("any" if plan is None else "%d%d" % plan),
    )(*args)


def pass_on(*refs):
    half = len(refs) // 2
    for a, b in zip(refs[:half], refs[half:]):
        b[...] = a[...]


def place(*arrays):
    specs = [
        pl.BlockSpec((1, 64, a.shape[2]), lambda i: (0, i, 0)) if a.ndim == 3
        else pl.BlockSpec((64, a.shape[1]), lambda i: (i, 0))
        for a in arrays
    ]
    return pl.pallas_call(
        pass_on,
        grid=(arrays[0].shape[0] // 64,),
        out_shape=tuple(jax.ShapeDtypeStruct(a.shape, a.dtype) for a in arrays),
        in_specs=specs,
        out_specs=tuple(specs),
        name="place",
    )(*arrays)


def local(tokens, expert_ids, gates, gate_weight, up_weight, down_weight, partner, capacity):
    rows, width = tokens.shape
    ff = gate_weight.shape[2]
    slots = jnp.arange(N, dtype=I32)
    ahead = jnp.remainder(partner // 4 - slots // 4, 4).reshape(4, 4)
    near = jnp.max(jnp.sum((ahead == 1).astype(I32), axis=1))
    far = jnp.max(jnp.sum((ahead == 2).astype(I32), axis=1))
    choice = jnp.int32(len(PLANS) - 1)
    for i, plan in reversed(list(enumerate(PLANS[:-1]))):
        choice = jnp.where((near <= plan[0]) & (far <= plan[1]), i, choice)
    args = (
        expert_ids.T, gates.T, capacity, partner, tokens.T,
        gate_weight, up_weight, down_weight.transpose(0, 2, 1),
    )
    mix, new_gate, new_up, new_down = lax.switch(
        choice, [functools.partial(layer, plan, rows, width, ff) for plan in PLANS], *args
    )
    mix, new_gate, new_up, new_down = place(mix, new_gate, new_up, new_down)
    return mix.T, new_gate, new_up, new_down.transpose(0, 2, 1)


def solution(mesh):
    return jax.shard_map(
        local,
        mesh=mesh,
        in_specs=(
            P("expert", "dp"),
            P("expert", None),
            P("expert", None),
            P("expert", "dp", None),
            P("expert", "dp", None),
            P("expert", None, "dp"),
            P(),
            P(),
        ),
        out_specs=(
            P("expert", "dp"),
            P("expert", "dp", None),
            P("expert", "dp", None),
            P("expert", None, "dp"),
        ),
        check_vma=False,
    )
```
